32 devices in a mesh: freq: 4 (over y, x), tile: 8 (over z, core).
Axes of the slice: x: 2, y: 2, z: 4, core: 2. Of those that a mesh axis runs over, the one named last changes fastest.
Arguments:
- voltages: bfloat16 [4096, 24960], P(('freq', 'tile')), may hold values from -16 to 16, as said below
- channel_ids: int32 [12], replicated, may hold values from 1 to 63
- start_basis: float32 [2, 8, 4096], replicated, may hold values from -0.0625 to 0.0625
Outputs:
- cleaned: float32 [2, 12, 192, 4096], P(None, 'freq', 'tile')
The draws below stay inside these ranges and needn't reach their ends.
Inputs may be any that keep to these rules, and one draw needn't show every extreme that they name: `voltages`: real samples of each input over the whole window.
All inputs are finite; a program needn't handle non-finite values.
Results may differ from the reference program's by a relative error of at most 0.0048.
Values may be sent and summed in bfloat16 or wider, within the bound.
A program may use at most 128 MiB of HBM per device.

```python
import math
import jax
import jax.numpy as jnp
from jax import lax

INPUTS = 4096
TAPS = 4
P_SIZE = 128
KDIM = 8
ITERS = 3
CHANNELS = 12
SPECTRA = 192
SAMPLES = 24960


highest = lax.Precision.HIGHEST


def draw_voltages(key, part):
    key_gain = jax.random.fold_in(key, 11)
    key_signal = jax.random.fold_in(key, 12)
    key_power = jax.random.fold_in(key, 13)
    key_noise = jax.random.fold_in(key, 14)
    sources = KDIM + 2
    powers = jnp.exp(jax.random.uniform(key_power, (sources,), jnp.float32, math.log(0.001), math.log(0.2)))
    time_frac = jnp.arange(SAMPLES, dtype=jnp.float32) / SAMPLES
    envelope = 0.6 + 1.2 * time_frac
    signals = jax.random.normal(key_signal, (sources, SAMPLES), jnp.float32) * jnp.sqrt(powers)[:, None] * envelope[None, :]
    gain_table = jax.random.normal(key_gain, (INPUTS, sources), jnp.float32)
    block_rows = min(INPUTS, 128)
    block_count = INPUTS // block_rows

    def one_block(block_at):
        first_row = block_at * block_rows
        gain_rows = lax.dynamic_slice_in_dim(gain_table, first_row, block_rows, 0)
        fraction = (first_row + jnp.arange(block_rows, dtype=jnp.int32)).astype(jnp.float32) / INPUTS
        noise_key = jax.random.fold_in(key_noise, block_at)
        noise_draw = jax.random.normal(noise_key, (block_rows, SAMPLES), jnp.float32)
        amplitude = 0.5 + fraction
        combined = amplitude[:, None] * (noise_draw + jnp.dot(gain_rows, signals, precision=highest))
        return jnp.clip(combined, -16.0, 16.0).astype(jnp.bfloat16)
    blocks = lax.map(one_block, jnp.arange(block_count, dtype=jnp.int32))
    return blocks.reshape(INPUTS, SAMPLES)


def place_ends(drawn, rng, low, top_value):
    longest = drawn.shape.index(max(drawn.shape))
    spots = []
    for shift in (0, 1):
        where = [jax.random.randint(jax.random.fold_in(rng, axis), (), 0, length) for axis, length in enumerate(drawn.shape)]
        where[longest] = (where[longest] + shift) % drawn.shape[longest]
        spots.append(tuple(where))
    return drawn.at[spots[0]].set(low).at[spots[1]].set(top_value)


def centred(rng, shape, spread, limit, kind=jnp.bfloat16):
    values = jax.random.normal(rng, shape, jnp.float32) * spread
    return jnp.minimum(jnp.maximum(values, -limit), limit).astype(kind)


def setup_inputs(seed: int = 0) -> dict:
    seeds = jax.random.split(jax.random.key(seed), 4)
    voltages = draw_voltages(jax.random.fold_in(seeds[3], 71), 0)
    channel_ids = place_ends(jax.random.randint(seeds[1], (CHANNELS,), 1, P_SIZE // 2), jax.random.fold_in(seeds[1], 1), 1, (P_SIZE // 2) - 1).astype(jnp.int32)
    start_basis = centred(seeds[2], (2, KDIM, INPUTS), (2 * INPUTS) ** -0.5, 0.0625, jnp.float32)
    return dict(voltages=voltages, channel_ids=channel_ids, start_basis=start_basis)


loading = 0.5
highest = lax.Precision.HIGHEST

def make_table(channel_ids, taps_count, points):
    length = taps_count * points
    offsets = jnp.arange(length, dtype=jnp.float32)
    shifted = (offsets + 0.5 - length / 2.0) / points
    window = jnp.sinc(shifted) * (0.5 - 0.5 * jnp.cos(2.0 * math.pi * (offsets + 0.5) / length))
    window = window / jnp.sqrt(jnp.sum(window * window))
    window = window.reshape(taps_count, points)
    phases = channel_ids[:, None] * jnp.arange(points, dtype=jnp.int32)[None, :] % points
    angles = 2.0 * math.pi / points * phases.astype(jnp.float32)
    rotors = jnp.stack([jnp.cos(angles), -jnp.sin(angles)])
    return (window[:, None, None, :] * rotors[None]).astype(jnp.bfloat16)

def channelize(voltages, coeffs):
    block_rows = min(INPUTS, 128)
    block_count = INPUTS // block_rows
    filter_table = coeffs.astype(jnp.float32)

    def one_block(first_row):
        chosen = lax.dynamic_slice_in_dim(voltages, first_row, block_rows, 0)
        frames = chosen.reshape(block_rows, SPECTRA + TAPS - 1, P_SIZE).astype(jnp.float32)
        summed = jnp.zeros((2, CHANNELS, SPECTRA, block_rows), jnp.float32)
        for offset in range(TAPS):
            summed = summed + jnp.einsum('rcp,isp->rcsi', filter_table[offset], frames[:, offset:offset + SPECTRA, :], precision=highest)
        return summed.astype(jnp.bfloat16)
    starts = (jnp.arange(block_count) * block_rows).astype(jnp.int32)
    stacked = lax.map(one_block, starts)
    return jnp.transpose(stacked, (1, 2, 3, 0, 4)).reshape(2, CHANNELS, SPECTRA, INPUTS)

def contract(form, left, right):
    return jnp.einsum(form, left, right, precision=highest)

def image_of(values, basis):
    real_v, imag_v = (values[0], values[1])
    real_q, imag_q = (basis[0], basis[1])
    weight_re = contract('csi,cki->csk', real_v, real_q) + contract('csi,cki->csk', imag_v, imag_q)
    weight_im = contract('csi,cki->csk', real_v, imag_q) - contract('csi,cki->csk', imag_v, real_q)
    image_re = contract('csi,csk->cki', real_v, weight_re) - contract('csi,csk->cki', imag_v, weight_im)
    image_im = contract('csi,csk->cki', real_v, weight_im) + contract('csi,csk->cki', imag_v, weight_re)
    return jnp.stack([image_re, image_im])

def gram_parts(image):
    real_z, imag_z = (image[0], image[1])
    gram_re = contract('cki,cji->ckj', real_z, real_z) + contract('cki,cji->ckj', imag_z, imag_z)
    gram_im = contract('cki,cji->ckj', real_z, imag_z) - contract('cki,cji->ckj', imag_z, real_z)
    return (gram_re, gram_im)

def lower_factor(gram_re, gram_im):
    basis_width = gram_re.shape[-1]
    lower_re = {}
    lower_im = {}
    pivots = []
    for column in range(basis_width):
        pivot_square = gram_re[:, column, column]
        for earlier in range(column):
            pivot_square = pivot_square - lower_re[column, earlier] ** 2 - lower_im[column, earlier] ** 2
        pivot_value = jnp.sqrt(pivot_square)
        pivots.append(pivot_value)
        for row_at in range(column + 1, basis_width):
            value_re = gram_re[:, row_at, column]
            value_im = gram_im[:, row_at, column]
            for earlier in range(column):
                left_re, left_im = (lower_re[row_at, earlier], lower_im[row_at, earlier])
                right_re, right_im = (lower_re[column, earlier], lower_im[column, earlier])
                value_re = value_re - (left_re * right_re + left_im * right_im)
                value_im = value_im - (left_im * right_re - left_re * right_im)
            lower_re[row_at, column] = value_re / pivot_value
            lower_im[row_at, column] = value_im / pivot_value
    return (lower_re, lower_im, pivots)

def apply_factor(image, lower_re, lower_im, pivots):
    basis_width = image.shape[2]
    result_re = []
    result_im = []
    for column in range(basis_width):
        value_re = image[0, :, column, :]
        value_im = image[1, :, column, :]
        for earlier in range(column):
            left_re, left_im = (result_re[earlier], result_im[earlier])
            right_re = lower_re[column, earlier][:, None]
            right_im = lower_im[column, earlier][:, None]
            value_re = value_re - (left_re * right_re + left_im * right_im)
            value_im = value_im - (left_im * right_re - left_re * right_im)
        divisor = pivots[column][:, None]
        result_re.append(value_re / divisor)
        result_im.append(value_im / divisor)
    return jnp.stack([jnp.stack(result_re, axis=1), jnp.stack(result_im, axis=1)])

def remove_subspace(values, basis):
    real_v, imag_v = (values[0], values[1])
    real_q, imag_q = (basis[0], basis[1])
    coord_re = contract('cki,csi->cks', real_q, real_v) + contract('cki,csi->cks', imag_q, imag_v)
    coord_im = contract('cki,csi->cks', real_q, imag_v) - contract('cki,csi->cks', imag_q, real_v)
    fitted_re = contract('cki,cks->csi', real_q, coord_re) - contract('cki,cks->csi', imag_q, coord_im)
    fitted_im = contract('cki,cks->csi', real_q, coord_im) + contract('cki,cks->csi', imag_q, coord_re)
    return values - jnp.stack([fitted_re, fitted_im])

def reference(voltages, channel_ids, start_basis):
    coeffs = make_table(channel_ids, TAPS, P_SIZE)
    spectra = channelize(voltages, coeffs)
    values = spectra.astype(jnp.float32)
    basis = jnp.broadcast_to(start_basis[:, None], (2, CHANNELS, KDIM, INPUTS))
    for step_at in range(ITERS):
        image = image_of(values, basis) / SPECTRA + loading * basis
        gram_re, gram_im = gram_parts(image)
        lower_re, lower_im, pivots = lower_factor(gram_re, gram_im)
        basis = apply_factor(image, lower_re, lower_im, pivots)
    return remove_subspace(values, basis)
```

```python
import functools
import math

import jax
import jax.numpy as jnp
from jax import lax
from jax.experimental import pallas as pl
from jax.experimental.pallas import tpu as pltpu
from jax.sharding import PartitionSpec as P

TAPS = 4
P_SIZE = 128
ITERS = 3
STEP = 16
SUB = 8
LAG = 4

loading = 0.5
highest = lax.Precision.HIGHEST
VMEM = pl.BlockSpec(memory_space=pltpu.VMEM)
MESH = pl.DeviceIdType.MESH


def make_table(channel_ids, taps_count, points):
    length = taps_count * points
    offsets = jnp.arange(length, dtype=jnp.float32)
    shifted = (offsets + 0.5 - length / 2.0) / points
    window = jnp.sinc(shifted) * (0.5 - 0.5 * jnp.cos(2.0 * math.pi * (offsets + 0.5) / length))
    window = window / jnp.sqrt(jnp.sum(window * window))
    window = window.reshape(taps_count, points)
    phases = channel_ids[:, None] * jnp.arange(points, dtype=jnp.int32)[None, :] % points
    angles = 2.0 * math.pi / points * phases.astype(jnp.float32)
    rotors = jnp.stack([jnp.cos(angles), -jnp.sin(angles)])
    return (window[:, None, None, :] * rotors[None]).astype(jnp.bfloat16)


def banded(coeffs):
    rows = coeffs.shape[1]
    spect = lax.broadcasted_iota(jnp.int32, (1, STEP, STEP + TAPS - 1, 1), 1)
    frame = lax.broadcasted_iota(jnp.int32, (1, STEP, STEP + TAPS - 1, 1), 2)
    table = jnp.zeros((rows, STEP, STEP + TAPS - 1, P_SIZE), jnp.bfloat16)
    for tap in range(TAPS):
        table = jnp.where(frame - spect == tap, coeffs[tap][:, None, None, :], table)
    return table.reshape(rows * STEP, (STEP + TAPS - 1) * P_SIZE)


def nt(left, right):
    return lax.dot_general(left, right, (((1,), (1,)), ((), ())), preferred_element_type=jnp.float32)


def split3(value):
    high = value.astype(jnp.bfloat16)
    rest = value - high.astype(jnp.float32)
    mid = rest.astype(jnp.bfloat16)
    low = (rest - mid.astype(jnp.float32)).astype(jnp.bfloat16)
    return jnp.concatenate([high, mid, low], axis=0)


def fold3(value):
    rows = value.shape[0] // 3
    return value[:rows] + value[rows : 2 * rows] + value[2 * rows :]


def plain(left, right):
    return lax.dot_general(left, right, (((1,), (0,)), ((), ())), preferred_element_type=jnp.float32)


def project(z, real_v, imag_v, k):
    parts = split3(z)
    on_re = fold3(nt(parts, real_v))
    on_im = fold3(nt(parts, imag_v))
    return jnp.concatenate([on_re[:k] + on_im[k:], on_re[k:] - on_im[:k]], axis=0)


def inverse_factor(gram, k, off=0):
    lanes = gram.shape[1]
    col = lax.broadcasted_iota(jnp.int32, (k, lanes), 1)
    row = lax.broadcasted_iota(jnp.int32, (k, lanes), 0)
    zero = jnp.zeros((k, lanes), jnp.float32)
    a_re = gram[:k]
    a_im = gram[k:]
    m_re = jnp.where(col == row, 1.0, zero)
    m_im = zero
    for j in range(k):
        at_col = col == j + off
        c_re = jnp.sum(jnp.where(at_col, a_re, 0.0), axis=1, keepdims=True)
        c_im = jnp.sum(jnp.where(at_col, a_im, 0.0), axis=1, keepdims=True)
        pivot = jnp.sqrt(c_re[j : j + 1])
        l_re = jnp.where(row[:, :1] > j, c_re / pivot, 0.0)
        l_im = jnp.where(row[:, :1] > j, c_im / pivot, 0.0)
        ar, ai = a_re[j : j + 1] / pivot, a_im[j : j + 1] / pivot
        mr, mi = m_re[j : j + 1] / pivot, m_im[j : j + 1] / pivot
        here = row == j
        a_re = jnp.where(here, ar, a_re - (l_re * ar - l_im * ai))
        a_im = jnp.where(here, ai, a_im - (l_re * ai + l_im * ar))
        m_re = jnp.where(here, mr, m_re - (l_re * mr - l_im * mi))
        m_im = jnp.where(here, mi, m_im - (l_re * mi + l_im * mr))
    return m_re, -m_im


def mix(m_re, m_im, rows, k):
    out_re = jnp.zeros((k, rows.shape[1]), jnp.float32)
    out_im = jnp.zeros((k, rows.shape[1]), jnp.float32)
    for j in range(k):
        f_re, f_im = m_re[:, j : j + 1], m_im[:, j : j + 1]
        r_re, r_im = rows[j : j + 1], rows[k + j : k + j + 1]
        out_re = out_re + (f_re * r_re - f_im * r_im)
        out_im = out_im + (f_re * r_im + f_im * r_re)
    return jnp.concatenate([out_re, out_im], axis=0)


def tn(left, right):
    return lax.dot_general(left, right, (((0,), (0,)), ((), ())), preferred_element_type=jnp.float32)


def fused_kernel(
    volts_hbm, ids_ref, start_ref, own_ref, q_ref, left_ref,
    vol_ref, table_ref, stage, v_ref, parts_ref, pack_ref, pair_ref, half_ref, land_ref, full_ref, res_ref,
    vol_sem, own_sem, mine_sem, f_send, f_recv, z_send, z_recv,
    p_send, p_recv, k_send, k_recv, j_send, j_recv, b_send, b_recv,
    up_send, down_send, line_recv, mate_send, mate_recv,
    *, k, freq, tile,
):
    chans, _, spectra, width = parts_ref.shape
    cols = vol_ref.shape[1]
    block = spectra // tile
    rows = 2 * block
    subs = block // SUB
    window = vol_ref.shape[2]
    group = lax.axis_index("freq")
    me = lax.axis_index("tile")
    line = tile // 2
    z, core = me // 2, lax.rem(me, 2)
    mate = me + 1 - 2 * core
    barrier = pltpu.get_barrier_semaphore()
    for d in range(1, freq):
        pl.semaphore_signal(barrier, inc=1, device_id={"freq": lax.rem(group + d, freq)}, device_id_type=MESH)
    for d in range(1, tile):
        pl.semaphore_signal(barrier, inc=1, device_id={"tile": lax.rem(me + d, tile)}, device_id_type=MESH)

    def remote(src, dst, send, recv, where):
        return pltpu.make_async_remote_copy(
            src_ref=src, dst_ref=dst, send_sem=send, recv_sem=recv, device_id=where, device_id_type=MESH
        )

    def block_at(j):
        return lax.rem(j, 2) * (tile // 2) + j // 2

    def fetch(j):
        lanes = pl.ds(pl.multiple_of(block_at(j) * (block * P_SIZE), P_SIZE), window)
        return pltpu.make_async_copy(volts_hbm.at[:, lanes], vol_ref.at[j], vol_sem.at[j])

    for j in range(tile):
        fetch(j).start()

    build_table(ids_ref, table_ref)
    pl.semaphore_wait(barrier, freq - 1 + tile - 1)

    def rows_of(b):
        return pl.ds(pl.multiple_of(b * rows, rows), rows)

    my_cols = pl.ds(pl.multiple_of(group * cols, cols), cols)

    def handover(j, d):
        peer = lax.rem(group + d, freq)
        return remote(
            stage.at[j, peer], v_ref.at[:, rows_of(block_at(j)), my_cols],
            f_send.at[j, d - 1], f_recv.at[j, d - 1], {"freq": peer},
        )

    def own_part(j):
        return pltpu.make_async_copy(
            stage.at[j, group], v_ref.at[:, rows_of(block_at(j)), my_cols], own_sem.at[j]
        )

    def filter_step(j):
        fetch(j).wait()
        span = (SUB + TAPS - 1) * P_SIZE
        right = jnp.concatenate(
            [vol_ref[j, :, n * SUB * P_SIZE : n * SUB * P_SIZE + span] for n in range(subs)], axis=0
        )
        result = nt(table_ref[...], right)
        pieces = [result[:, n * cols : (n + 1) * cols].reshape(-1, SUB, cols) for n in range(subs)]
        result = jnp.concatenate(pieces, axis=1)
        stage[j] = result.reshape(freq, chans, rows, cols).astype(jnp.bfloat16)
        for d in range(1, freq):
            handover(j, d).start()
        own_part(j).start()

    def arrive(j):
        for d in range(1, freq):
            handover(j, d).wait_recv()
        own_part(j).wait()

    def forward(b):
        return remote(v_ref.at[:, rows_of(b), :], own_ref.at[me], z_send.at[b], z_recv.at[me], {"tile": b})

    def keep(b):
        return pltpu.make_async_copy(v_ref.at[:, rows_of(b), :], own_ref.at[me], mine_sem)

    def pass_on(j):
        b = block_at(j)

        @pl.when(b != me)
        def _():
            forward(b).start()

        @pl.when(b == me)
        def _():
            keep(b).start()

    def first(j, carry):
        filter_step(j)
        return carry

    def both(j, carry):
        filter_step(j)
        arrive(j - LAG)
        pass_on(j - LAG)
        return carry

    def last(j, carry):
        arrive(j)
        return carry

    lax.fori_loop(0, LAG, first, 0)
    lax.fori_loop(LAG, tile, both, 0)
    lax.fori_loop(tile - LAG, tile, last, 0)

    start = jnp.concatenate(
        [
            start_ref[:, pl.ds(pl.multiple_of(f * (tile * cols) + me * cols, cols), cols)]
            for f in range(freq)
        ],
        axis=1,
    )
    start3 = split3(start)
    fold = spectra - 128
    half = pack_ref.shape[2]
    keep_mask = lax.broadcasted_iota(jnp.int32, (spectra, spectra), 0) >= lax.broadcasted_iota(
        jnp.int32, (spectra, spectra), 1
    )
    pad_lanes = 128 - fold

    def folded(value):
        count = value.shape[0] // 2
        wide = jnp.concatenate([value[:, 128:], jnp.zeros((2 * count, pad_lanes), jnp.float32)], axis=1)
        return wide[:count] + pltpu.roll(wide[count:], fold, 1)

    def to_mate(c):
        return remote(pack_ref.at[c, 1 - core], pair_ref.at[c], p_send.at[c], p_recv.at[c], {"tile": mate})

    for c in range(chans):
        loose = v_ref[c].astype(jnp.float32).reshape(tile, 2, block, width)
        real_v = loose[:, 0].reshape(spectra, width).astype(jnp.bfloat16)
        imag_v = loose[:, 1].reshape(spectra, width).astype(jnp.bfloat16)
        parts_ref[c, 0] = real_v
        parts_ref[c, 1] = imag_v
        k_re = nt(real_v, real_v) + nt(imag_v, imag_v)
        k_im = nt(real_v, imag_v) - nt(imag_v, real_v)
        packed = jnp.where(keep_mask, k_re, k_im)
        on_re = fold3(nt(start3, real_v))
        on_im = fold3(nt(start3, imag_v))
        w = jnp.concatenate([on_re[:k] + on_im[k:], on_re[k:] - on_im[:k]], axis=0)
        tail = 2 * half - (spectra + spectra // 2 + 3 * k)
        everything = jnp.concatenate(
            [packed[:, :128], folded(packed), w[:, :128], folded(w), jnp.zeros((tail, 128), jnp.float32)], axis=0
        )
        pack_ref[c] = everything.reshape(2, half, 128)
        to_mate(c).start()

    def root_line(c):
        return line // 2 - 1 + c % 2

    def to_root(c, d):
        return remote(
            half_ref.at[c], land_ref.at[c, d - 1], k_send.at[c], k_recv.at[c, d - 1],
            {"tile": 2 * root_line(c) + core},
        )

    for c in range(chans):
        to_mate(c).wait_recv()
        half_ref[c] = pack_ref[c, core] + pair_ref[c]
        for d in range(1, line):

            @pl.when(z == (root_line(c) + d) % line)
            def _():
                to_root(c, d).start()

    for j in range(tile - LAG, tile):
        pass_on(j)

    g_re = exact(start_ref[...], start_ref[:k])
    g_im = exact(start_ref[...], start_ref[k:])
    gram0 = jnp.concatenate([g_re[:k] + g_im[k:], g_im[:k] - g_re[k:]], axis=0)

    def join(c):
        return remote(half_ref.at[c], full_ref.at[core], j_send.at[c], j_recv.at[c], {"tile": mate})

    for c in range(chans):

        @pl.when(z == root_line(c))
        def _():
            total = half_ref[c]
            for d in range(1, line):
                to_root(c, d).wait_recv()
                total = total + land_ref[c, d - 1]

            @pl.when(core == c // 2)
            def _():
                full_ref[core] = total

            @pl.when(core != c // 2)
            def _():
                half_ref[c] = total
                join(c).start()

    side = z - (line // 2 - 1)
    at = side + 2 * core
    is_root = (side >= 0) & (side < 2) & (at < chans)

    def spread(c, d):
        return remote(
            res_ref.at[c], res_ref.at[c], b_send.at[d - 1], b_recv.at[c], {"tile": lax.rem(me + d, tile)}
        )

    @pl.when(is_root)
    def _():
        for c in range(chans):

            @pl.when(at == c)
            def _():
                join(c).wait_recv()

        res_ref[at] = iterate(full_ref[...].reshape(2 * half, 128), gram0, k, spectra)
        for d in range(1, tile):
            spread(at, d).start()

    def line_copy(c, origin, to, sem):
        slot = 2 * origin + core
        return remote(
            q_ref.at[slot, c], q_ref.at[slot, c], sem.at[c, origin], line_recv.at[c, origin], {"tile": 2 * to + core}
        )

    def mate_copy(c, origin):
        slot = 2 * origin + core
        return remote(
            q_ref.at[slot, c], q_ref.at[slot, c], mate_send.at[c, origin], mate_recv.at[c, origin], {"tile": mate}
        )

    def send_on(c, origin, up, down):
        if up:

            @pl.when(z < line - 1)
            def _():
                line_copy(c, origin, z + 1, up_send).start()

        if down:

            @pl.when(z > 0)
            def _():
                line_copy(c, origin, z - 1, down_send).start()

        mate_copy(c, origin).start()

    for c in range(chans):

        @pl.when(jnp.logical_not(is_root & (at == c)))
        def _():
            spread(c, 1).wait_recv()

        w = res_ref[c, :, :spectra]
        a = res_ref[c, :, 256 : 256 + spectra]
        b = res_ref[c, :, 512:640]
        parts = split3(a)
        on_re = fold3(plain(parts, parts_ref[c, 0]))
        on_im = fold3(plain(parts, parts_ref[c, 1]))
        q = jnp.concatenate([on_re[:k] - on_im[k:], on_re[k:] + on_im[:k]], axis=0)
        q_ref[me, c] = q + mix(b[:k], b[k:], start, k)
        send_on(c, z, True, True)
        turned = jnp.concatenate([-w[k:], w[:k]], axis=0)
        chosen = jnp.zeros((2 * k, rows), jnp.float32)
        for t in range(tile):
            lanes = slice(t * block, (t + 1) * block)
            pair = jnp.concatenate([w[:, lanes], turned[:, lanes]], axis=1)
            chosen = jnp.where(me == t, pair, chosen)
        left_ref[c] = chosen

    for d in range(1, line):
        for c in range(chans):

            @pl.when(z >= d)
            def _():
                line_copy(c, z - d, z, up_send).wait_recv()
                send_on(c, z - d, True, False)

            @pl.when(z + d < line)
            def _():
                line_copy(c, z + d, z, down_send).wait_recv()
                send_on(c, z + d, False, True)

    for c in range(chans):
        for origin in range(line):
            mate_copy(c, origin).wait()

            @pl.when((z >= origin) & (z < line - 1))
            def _():
                line_copy(c, origin, z + 1, up_send).wait_send()

            @pl.when((z <= origin) & (z > 0))
            def _():
                line_copy(c, origin, z - 1, down_send).wait_send()

    def drain(j, carry):
        for d in range(1, freq):
            handover(j, d).wait_send()

        @pl.when(j != me)
        def _():
            forward(j).wait_send()
            remote(v_ref.at[:, rows_of(j), :], own_ref.at[j], z_send.at[j], z_recv.at[j], {"tile": j}).wait_recv()

        @pl.when(j == me)
        def _():
            keep(j).wait()

        return carry

    lax.fori_loop(0, tile, drain, 0)
    for c in range(chans):
        to_mate(c).wait_send()

        @pl.when(z != root_line(c))
        def _():
            to_root(c, 1).wait_send()

        @pl.when((z == root_line(c)) & (core != c // 2))
        def _():
            join(c).wait_send()

    @pl.when(is_root)
    def _():
        for d in range(1, tile):
            spread(at, d).wait_send()


def exact(left, right):
    return lax.dot_general(
        left, right, (((1,), (1,)), ((), ())), precision=highest, preferred_element_type=jnp.float32
    )


def build_table(ids_ref, table_ref):
    count = ids_ref.shape[0]
    length = TAPS * P_SIZE
    tap = lax.broadcasted_iota(jnp.int32, (8, P_SIZE), 0)
    point = lax.broadcasted_iota(jnp.int32, (8, P_SIZE), 1)
    offsets = (tap * P_SIZE + point).astype(jnp.float32)
    shifted = math.pi * ((offsets + 0.5 - length / 2.0) / P_SIZE)
    shape = jnp.sin(shifted) / shifted
    shape = shape * (0.5 - 0.5 * jnp.cos(2.0 * math.pi * (offsets + 0.5) / length))
    shape = jnp.where(tap < TAPS, shape, 0.0)
    total = jnp.sum(jnp.sum(shape * shape, axis=1, keepdims=True), axis=0, keepdims=True)
    shape = shape / jnp.sqrt(total)
    part = lax.broadcasted_iota(jnp.int32, (count, P_SIZE), 0)
    place = lax.broadcasted_iota(jnp.int32, (count, P_SIZE), 1)
    phases = jnp.bitwise_and(ids_ref[...] * place, P_SIZE - 1)
    angles = 2.0 * math.pi / P_SIZE * phases.astype(jnp.float32)
    rotors = jnp.where(jnp.bitwise_and(part, 1) == 0, jnp.cos(angles), -jnp.sin(angles))
    spread = []
    for m in range(TAPS):
        taps = rotors * shape[m : m + 1]
        spread.append(jnp.broadcast_to(taps[:, None, :], (count, SUB, P_SIZE)))
    at = lax.broadcasted_iota(jnp.int32, (count, SUB, P_SIZE), 1)
    for frame in range(SUB + TAPS - 1):
        value = jnp.zeros((count, SUB, P_SIZE), jnp.float32)
        for m in range(TAPS):
            if 0 <= frame - m < SUB:
                value = jnp.where(at == frame - m, spread[m], value)
        table_ref[:, frame * P_SIZE : (frame + 1) * P_SIZE] = value.reshape(count * SUB, P_SIZE).astype(jnp.bfloat16)


def iterate(full, gram0, k, spectra):
    fold = spectra - 128
    count = spectra // 2
    lane = lax.broadcasted_iota(jnp.int32, (1, 128), 1)

    def unfold(top, bent):
        low = jnp.where(lane < fold, bent, 0.0)
        high = jnp.where(lane < fold, pltpu.roll(bent, 128 - fold, 1), 0.0)
        return jnp.concatenate([top, jnp.concatenate([low, high], axis=0)], axis=1)

    packed = unfold(full[:spectra], full[spectra : spectra + count])
    at = spectra + count
    w = unfold(full[at : at + 2 * k], full[at + 2 * k : at + 3 * k])
    packed = jnp.concatenate([packed, jnp.zeros((256 - spectra, 256), jnp.float32)], axis=0)
    turned = packed.T
    row = lax.broadcasted_iota(jnp.int32, (256, 256), 0)
    col = lax.broadcasted_iota(jnp.int32, (256, 256), 1)
    k_re = jnp.where(row >= col, packed, turned)
    k_im = jnp.where(row < col, packed, jnp.where(row > col, -turned, 0.0))
    both = jnp.concatenate([k_re, k_im], axis=1)
    high = both.astype(jnp.bfloat16)
    rest = both - high.astype(jnp.float32)
    mid = rest.astype(jnp.bfloat16)
    low = (rest - mid.astype(jnp.float32)).astype(jnp.bfloat16)
    n2 = 2 * k
    a = jnp.zeros((n2, 256), jnp.float32)
    b = jnp.where(
        lax.broadcasted_iota(jnp.int32, (n2, 128), 0) == lax.broadcasted_iota(jnp.int32, (n2, 128), 1), 1.0, 0.0
    )
    b = jnp.where(lax.broadcasted_iota(jnp.int32, (n2, 128), 0) < k, b, 0.0)
    held = gram0
    for _ in range(ITERS):
        w3 = split3(w)
        on_high = plain(w3, high)
        on_mid = plain(w3[: 2 * n2], mid)
        on_low = plain(w3[:n2], low)
        kw = (on_low + on_mid[n2:] + on_high[2 * n2 :]) + (on_mid[:n2] + on_high[n2 : 2 * n2]) + on_high[:n2]
        on_re, on_im = kw[:, :256], kw[:, 256:]
        kw = jnp.concatenate([on_re[:k] + on_im[k:], on_re[k:] - on_im[:k]], axis=0)
        y = kw / spectra + loading * w
        u = (y + loading * w) / spectra
        g_re = exact(w, u[:k])
        g_im = exact(w, u[k:])
        gram = jnp.concatenate([g_re[:k] + g_im[k:], g_im[:k] - g_re[k:]], axis=0) + loading * loading * held
        m_re, m_im = inverse_factor(gram, k)
        grown = jnp.concatenate([y, w / spectra + loading * a, loading * b], axis=1)
        grown = mix(m_re, m_im, grown, k)
        w, a, b = grown[:, :256], grown[:, 256:512], grown[:, 512:]
        held = b_identity(n2, k)
    return jnp.concatenate([w, a, b], axis=1)


def b_identity(n2, k):
    row = lax.broadcasted_iota(jnp.int32, (n2, k), 0)
    col = lax.broadcasted_iota(jnp.int32, (n2, k), 1)
    return jnp.where(row == col, 1.0, 0.0)


def finish_kernel(own_ref, q_ref, left_ref, out_ref):
    tile, chans, rows, cols = own_ref.shape
    block = rows // 2
    n2 = q_ref.shape[2]
    for c in range(chans):
        w3 = split3(left_ref[c])
        w_left = jnp.concatenate([w3[:n2], w3[:n2], w3[n2 : 2 * n2], w3[n2 : 2 * n2], w3[:n2], w3[2 * n2 :]], axis=0)
        for t in range(tile):
            s3 = split3(q_ref[t, c])
            s_right = jnp.concatenate(
                [s3[:n2], s3[n2 : 2 * n2], s3[:n2], s3[n2 : 2 * n2], s3[2 * n2 :], s3[:n2]], axis=0
            )
            cleaned = own_ref[t, c].astype(jnp.float32) - tn(w_left, s_right)
            out_ref[0, c, :, t * cols : (t + 1) * cols] = cleaned[:block]
            out_ref[1, c, :, t * cols : (t + 1) * cols] = cleaned[block:]


def channelize_kernel(volts_ref, table_ref, out_ref):
    step = pl.program_id(0)
    span = (STEP + TAPS - 1) * P_SIZE
    start = pl.multiple_of(step * (STEP * P_SIZE), P_SIZE)
    chunk = volts_ref[:, pl.ds(start, span)]
    result = nt(table_ref[...], chunk)
    out_ref[...] = result.reshape(out_ref.shape).astype(jnp.bfloat16)


def channelize(voltages, table, rows, spectra_all):
    inputs_local, samples = voltages.shape
    return pl.pallas_call(
        channelize_kernel,
        grid=(spectra_all // STEP,),
        in_specs=[VMEM, VMEM],
        out_specs=pl.BlockSpec((rows, STEP, inputs_local), lambda i: (0, i, 0)),
        out_shape=jax.ShapeDtypeStruct((rows, spectra_all, inputs_local), jnp.bfloat16),
        compiler_params=pltpu.CompilerParams(vmem_limit_bytes=40 * 2**20),
    )(voltages, table)


def start_kernel(v_ref, q_ref, pg_ref, *, k, lanes):
    chans, _, spectra, _ = v_ref.shape
    pg_ref[...] = jnp.zeros_like(pg_ref)
    for c in range(chans):
        pg_ref[2 * k * c : 2 * k * (c + 1), :spectra] = project(q_ref[...], v_ref[c, 0], v_ref[c, 1], k)


def step_kernel(v_ref, z_ref, pg_ref, z_out, pg_out, *, k, lanes, first):
    chans, _, spectra, width = v_ref.shape
    pg_out[...] = jnp.zeros_like(pg_out)
    for c in range(chans):
        at = slice(2 * k * c, 2 * k * (c + 1))
        weights = pg_ref[at, :spectra]
        basis = z_ref[...] if first else z_ref[c]
        if not first:
            m_re, m_im = inverse_factor(pg_ref[at, lanes:], k)
            weights = mix(m_re, m_im, weights, k)
            basis = mix(m_re, m_im, basis, k)
        real_v, imag_v = v_ref[c, 0], v_ref[c, 1]
        parts = split3(weights / spectra)
        on_re = fold3(plain(parts, real_v))
        on_im = fold3(plain(parts, imag_v))
        z = jnp.concatenate([on_re[:k] - on_im[k:], on_re[k:] + on_im[:k]], axis=0) + loading * basis
        z_out[c] = z
        pg_out[at, :spectra] = project(z, real_v, imag_v, k)
        pad = jnp.zeros((lanes_pad(k), width), jnp.float32)
        right = jnp.concatenate([z[:k], pad], axis=0)
        right_im = jnp.concatenate([z[k:], pad], axis=0)
        dims = (((1,), (1,)), ((), ()))
        first_dot = lax.dot_general(z, right, dims, precision=highest, preferred_element_type=jnp.float32)
        second_dot = lax.dot_general(z, right_im, dims, precision=highest, preferred_element_type=jnp.float32)
        g_re = first_dot[:k] + second_dot[k:]
        g_im = second_dot[:k] - first_dot[k:]
        pg_out[at, lanes:] = jnp.concatenate([g_re, g_im], axis=0)


def lanes_pad(k):
    return 128 - k


def clean_kernel(v_ref, z_ref, pg_ref, out_ref, *, k, lanes):
    chans, _, spectra, width = v_ref.shape
    parts_count, _, _, block, _ = out_ref.shape
    for c in range(chans):
        at = slice(2 * k * c, 2 * k * (c + 1))
        m_re, m_im = inverse_factor(pg_ref[at, lanes:], k)
        w = mix(m_re, m_im, pg_ref[at, :spectra], k)
        q = mix(m_re, m_im, z_ref[c], k)
        turned = jnp.concatenate([q[k:], -q[:k]], axis=0)
        w3 = split3(w)
        n2 = 2 * k
        w_left = jnp.concatenate([w3[:n2], w3[:n2], w3[n2 : 2 * n2], w3[n2 : 2 * n2], w3[:n2], w3[2 * n2 :]], axis=0)
        for r, side in ((0, q), (1, turned)):
            s3 = split3(side)
            s_right = jnp.concatenate(
                [s3[:n2], s3[n2 : 2 * n2], s3[:n2], s3[n2 : 2 * n2], s3[2 * n2 :], s3[:n2]], axis=0
            )
            fitted = tn(w_left, s_right)
            cleaned = v_ref[c, r].astype(jnp.float32) - fitted
            out_ref[:, r, c] = cleaned.reshape(parts_count, block, width).astype(jnp.bfloat16)


def reduce_kernel(x_ref, out_ref, land_ref, send1, recv1, send2, recv2, *, size, chunk):
    me = lax.axis_index("tile")
    barrier = pltpu.get_barrier_semaphore()
    for d in range(1, size):
        peer = lax.rem(me + d, size)
        pl.semaphore_signal(barrier, inc=1, device_id={"tile": peer}, device_id_type=MESH)
    pl.semaphore_wait(barrier, size - 1)
    mine = pl.ds(pl.multiple_of(me * chunk, 8), chunk)
    sends = []
    for d in range(1, size):
        peer = lax.rem(me + d, size)
        copy = pltpu.make_async_remote_copy(
            src_ref=x_ref.at[pl.ds(pl.multiple_of(peer * chunk, 8), chunk)],
            dst_ref=land_ref.at[d - 1],
            send_sem=send1.at[d - 1],
            recv_sem=recv1.at[d - 1],
            device_id={"tile": peer},
            device_id_type=MESH,
        )
        copy.start()
        sends.append(copy)
    total = x_ref[mine]
    for d in range(1, size):
        sends[d - 1].wait_recv()
        total = total + land_ref[d - 1]
    out_ref[mine] = total
    later = []
    for d in range(1, size):
        peer = lax.rem(me + d, size)
        copy = pltpu.make_async_remote_copy(
            src_ref=out_ref.at[mine],
            dst_ref=out_ref.at[mine],
            send_sem=send2.at[d - 1],
            recv_sem=recv2.at[d - 1],
            device_id={"tile": peer},
            device_id_type=MESH,
        )
        copy.start()
        later.append(copy)
    for copy in later:
        copy.wait_recv()
    for copy in sends + later:
        copy.wait_send()


def tile_sum(x, size):
    rows, width = x.shape
    chunk = rows // size
    return pl.pallas_call(
        functools.partial(reduce_kernel, size=size, chunk=chunk),
        in_specs=[VMEM],
        out_specs=VMEM,
        out_shape=jax.ShapeDtypeStruct(x.shape, jnp.float32),
        scratch_shapes=[pltpu.VMEM((size - 1, chunk, width), jnp.float32)]
        + [pltpu.SemaphoreType.DMA((size - 1,))] * 4,
        compiler_params=pltpu.CompilerParams(collective_id=0, has_side_effects=True),
    )(x)


def up(value, unit):
    return -(-value // unit) * unit


def body_split(voltages, channel_ids, start_basis):
    inputs_local, samples_count = voltages.shape
    freq_count = lax.axis_size("freq")
    tile_count = lax.axis_size("tile")
    channels = channel_ids.shape[0]
    chan_local = channels // freq_count
    spectra_all = samples_count // P_SIZE - TAPS + 1
    spectra_local = spectra_all // tile_count
    k = start_basis.shape[1]
    width = freq_count * inputs_local

    coeffs = make_table(channel_ids, TAPS, P_SIZE).reshape(TAPS, 2 * channels, P_SIZE)
    local = channelize(voltages, banded(coeffs), 2 * channels, spectra_all)
    parcel = local.reshape(2, freq_count, chan_local, spectra_all, inputs_local)
    arrived = lax.all_to_all(parcel, "freq", split_axis=1, concat_axis=1, tiled=True)
    values = jnp.transpose(arrived, (2, 0, 3, 1, 4)).reshape(chan_local, 2, spectra_all, width)

    mine = lax.axis_index("tile")
    start = start_basis.reshape(2 * k, freq_count, tile_count, inputs_local)
    start = lax.dynamic_index_in_dim(start, mine, 2, keepdims=False).reshape(2 * k, width)

    lanes = up(spectra_all, 128)
    chunk = up(-(-chan_local * 2 * k // tile_count), 8)
    packed = jax.ShapeDtypeStruct((tile_count * chunk, lanes + 128), jnp.float32)
    z_shape = jax.ShapeDtypeStruct((chan_local, 2 * k, width), jnp.float32)
    params = pltpu.CompilerParams(vmem_limit_bytes=40 * 2**20)

    partial = pl.pallas_call(
        functools.partial(start_kernel, k=k, lanes=lanes),
        in_specs=[VMEM] * 2, out_specs=VMEM, out_shape=packed, compiler_params=params,
    )(values, start)
    z = start
    for step_at in range(ITERS):
        total = tile_sum(partial, tile_count)
        z, partial = pl.pallas_call(
            functools.partial(step_kernel, k=k, lanes=lanes, first=step_at == 0),
            in_specs=[VMEM] * 3, out_specs=[VMEM] * 2, out_shape=[z_shape, packed],
            compiler_params=params,
        )(values, z, total)
    total = tile_sum(partial, tile_count)
    cleaned = pl.pallas_call(
        functools.partial(clean_kernel, k=k, lanes=lanes),
        in_specs=[VMEM] * 3, out_specs=VMEM,
        out_shape=jax.ShapeDtypeStruct((tile_count, 2, chan_local, spectra_local, width), jnp.bfloat16),
        compiler_params=params,
    )(values, z, total)
    moved = lax.all_to_all(cleaned, "tile", split_axis=0, concat_axis=0, tiled=True)
    moved = moved.reshape(tile_count, 2, chan_local, spectra_local, freq_count, inputs_local)
    moved = jnp.transpose(moved, (1, 2, 3, 4, 0, 5)).astype(jnp.float32)
    return moved.reshape(2, chan_local, spectra_local, freq_count * tile_count * inputs_local)


def body(voltages, channel_ids, start_basis):
    inputs_local, samples_count = voltages.shape
    freq_count = lax.axis_size("freq")
    tile_count = lax.axis_size("tile")
    if inputs_local % 128:
        return body_split(voltages, channel_ids, start_basis)
    channels = channel_ids.shape[0]
    chan_local = channels // freq_count
    spectra_all = samples_count // P_SIZE - TAPS + 1
    spectra_local = spectra_all // tile_count
    k = start_basis.shape[1]
    width = freq_count * inputs_local
    if spectra_all != 192 or spectra_local % SUB or tile_count % 4 or chan_local > 4 or k != 8:
        return body_split(voltages, channel_ids, start_basis)

    ids = jnp.broadcast_to(jnp.repeat(channel_ids, 2)[:, None], (2 * channels, P_SIZE))
    start = start_basis.reshape(2 * k, freq_count * tile_count * inputs_local)
    rows = 2 * spectra_local
    line = tile_count // 2
    half = up(spectra_all + spectra_all // 2 + 3 * k, 16) // 2
    sem = pltpu.SemaphoreType.DMA
    peers = freq_count - 1
    own, q, left = pl.pallas_call(
        functools.partial(fused_kernel, k=k, freq=freq_count, tile=tile_count),
        in_specs=[pl.BlockSpec(memory_space=pl.ANY), VMEM, VMEM],
        out_specs=[pl.BlockSpec(memory_space=pl.ANY), VMEM, VMEM],
        out_shape=[
            jax.ShapeDtypeStruct((tile_count, chan_local, rows, width), jnp.bfloat16),
            jax.ShapeDtypeStruct((tile_count, chan_local, 2 * k, width), jnp.float32),
            jax.ShapeDtypeStruct((chan_local, 2 * k, rows), jnp.float32),
        ],
        scratch_shapes=[
            pltpu.VMEM((tile_count, inputs_local, (spectra_local + TAPS - 1) * P_SIZE), jnp.bfloat16),
            pltpu.VMEM((2 * channels * SUB, (SUB + TAPS - 1) * P_SIZE), jnp.bfloat16),
            pltpu.VMEM((tile_count, freq_count, chan_local, rows, inputs_local), jnp.bfloat16),
            pltpu.VMEM((chan_local, tile_count * rows, width), jnp.bfloat16),
            pltpu.VMEM((chan_local, 2, spectra_all, width), jnp.bfloat16),
            pltpu.VMEM((chan_local, 2, half, 128), jnp.float32),
            pltpu.VMEM((chan_local, half, 128), jnp.float32),
            pltpu.VMEM((chan_local, half, 128), jnp.float32),
            pltpu.VMEM((chan_local, line - 1, half, 128), jnp.float32),
            pltpu.VMEM((2, half, 128), jnp.float32),
            pltpu.VMEM((chan_local, 2 * k, 640), jnp.float32),
            sem((tile_count,)), sem((tile_count,)), sem(()),
            sem((tile_count, peers)), sem((tile_count, peers)),
            sem((tile_count,)), sem((tile_count,)),
            sem((chan_local,)), sem((chan_local,)),
            sem((chan_local,)), sem((chan_local, line - 1)),
            sem((chan_local,)), sem((chan_local,)),
            sem((tile_count - 1,)), sem((chan_local,)),
            sem((chan_local, line)), sem((chan_local, line)), sem((chan_local, line)),
            sem((chan_local, line)), sem((chan_local, line)),
        ],
        compiler_params=pltpu.CompilerParams(
            collective_id=0, has_side_effects=True, vmem_limit_bytes=56 * 2**20
        ),
    )(voltages, ids, start)
    stride = tile_count * inputs_local
    return pl.pallas_call(
        finish_kernel,
        grid=(freq_count,),
        in_specs=[
            pl.BlockSpec((tile_count, chan_local, rows, inputs_local), lambda f: (0, 0, 0, f)),
            pl.BlockSpec((tile_count, chan_local, 2 * k, inputs_local), lambda f: (0, 0, 0, f)),
            pl.BlockSpec((chan_local, 2 * k, rows), lambda f: (0, 0, 0)),
        ],
        out_specs=pl.BlockSpec((2, chan_local, spectra_local, stride), lambda f: (0, 0, 0, f)),
        out_shape=jax.ShapeDtypeStruct((2, chan_local, spectra_local, freq_count * stride), jnp.float32),
        compiler_params=pltpu.CompilerParams(vmem_limit_bytes=40 * 2**20),
    )(own, q, left)


def solution(mesh):
    in_specs = (P(("freq", "tile"), None), P(), P())
    out_specs = P(None, "freq", "tile", None)
    return jax.shard_map(body, mesh=mesh, in_specs=in_specs, out_specs=out_specs, check_vma=False)
```

```python
import functools
import math

import jax
import jax.numpy as jnp
from jax import lax
from jax.experimental import pallas as pl
from jax.experimental.pallas import tpu as pltpu
from jax.sharding import PartitionSpec as P

TAPS = 4
P_SIZE = 128
ITERS = 3
STEP = 16
SUB = 8
EARLY = 4

loading = 0.5
highest = lax.Precision.HIGHEST
VMEM = pl.BlockSpec(memory_space=pltpu.VMEM)
MESH = pl.DeviceIdType.MESH


def make_table(channel_ids, taps_count, points):
    length = taps_count * points
    offsets = jnp.arange(length, dtype=jnp.float32)
    shifted = (offsets + 0.5 - length / 2.0) / points
    window = jnp.sinc(shifted) * (0.5 - 0.5 * jnp.cos(2.0 * math.pi * (offsets + 0.5) / length))
    window = window / jnp.sqrt(jnp.sum(window * window))
    window = window.reshape(taps_count, points)
    phases = channel_ids[:, None] * jnp.arange(points, dtype=jnp.int32)[None, :] % points
    angles = 2.0 * math.pi / points * phases.astype(jnp.float32)
    rotors = jnp.stack([jnp.cos(angles), -jnp.sin(angles)])
    return (window[:, None, None, :] * rotors[None]).astype(jnp.bfloat16)


def banded(coeffs):
    rows = coeffs.shape[1]
    spect = lax.broadcasted_iota(jnp.int32, (1, STEP, STEP + TAPS - 1, 1), 1)
    frame = lax.broadcasted_iota(jnp.int32, (1, STEP, STEP + TAPS - 1, 1), 2)
    table = jnp.zeros((rows, STEP, STEP + TAPS - 1, P_SIZE), jnp.bfloat16)
    for tap in range(TAPS):
        table = jnp.where(frame - spect == tap, coeffs[tap][:, None, None, :], table)
    return table.reshape(rows * STEP, (STEP + TAPS - 1) * P_SIZE)


def nt(left, right):
    return lax.dot_general(left, right, (((1,), (1,)), ((), ())), preferred_element_type=jnp.float32)


def split3(value):
    high = value.astype(jnp.bfloat16)
    rest = value - high.astype(jnp.float32)
    mid = rest.astype(jnp.bfloat16)
    low = (rest - mid.astype(jnp.float32)).astype(jnp.bfloat16)
    return jnp.concatenate([high, mid, low], axis=0)


def fold3(value):
    rows = value.shape[0] // 3
    return value[:rows] + value[rows : 2 * rows] + value[2 * rows :]


def plain(left, right):
    return lax.dot_general(left, right, (((1,), (0,)), ((), ())), preferred_element_type=jnp.float32)


def project(z, real_v, imag_v, k):
    parts = split3(z)
    on_re = fold3(nt(parts, real_v))
    on_im = fold3(nt(parts, imag_v))
    return jnp.concatenate([on_re[:k] + on_im[k:], on_re[k:] - on_im[:k]], axis=0)


def inverse_factor(gram, k, off=0):
    lanes = gram.shape[1]
    col = lax.broadcasted_iota(jnp.int32, (k, lanes), 1)
    row = lax.broadcasted_iota(jnp.int32, (k, lanes), 0)
    zero = jnp.zeros((k, lanes), jnp.float32)
    a_re = gram[:k]
    a_im = gram[k:]
    m_re = jnp.where(col == row, 1.0, zero)
    m_im = zero
    for j in range(k):
        at_col = col == j + off
        c_re = jnp.sum(jnp.where(at_col, a_re, 0.0), axis=1, keepdims=True)
        c_im = jnp.sum(jnp.where(at_col, a_im, 0.0), axis=1, keepdims=True)
        pivot = jnp.sqrt(c_re[j : j + 1])
        l_re = jnp.where(row[:, :1] > j, c_re / pivot, 0.0)
        l_im = jnp.where(row[:, :1] > j, c_im / pivot, 0.0)
        ar, ai = a_re[j : j + 1] / pivot, a_im[j : j + 1] / pivot
        mr, mi = m_re[j : j + 1] / pivot, m_im[j : j + 1] / pivot
        here = row == j
        a_re = jnp.where(here, ar, a_re - (l_re * ar - l_im * ai))
        a_im = jnp.where(here, ai, a_im - (l_re * ai + l_im * ar))
        m_re = jnp.where(here, mr, m_re - (l_re * mr - l_im * mi))
        m_im = jnp.where(here, mi, m_im - (l_re * mi + l_im * mr))
    return m_re, -m_im


def mix(m_re, m_im, rows, k):
    out_re = jnp.zeros((k, rows.shape[1]), jnp.float32)
    out_im = jnp.zeros((k, rows.shape[1]), jnp.float32)
    for j in range(k):
        f_re, f_im = m_re[:, j : j + 1], m_im[:, j : j + 1]
        r_re, r_im = rows[j : j + 1], rows[k + j : k + j + 1]
        out_re = out_re + (f_re * r_re - f_im * r_im)
        out_im = out_im + (f_re * r_im + f_im * r_re)
    return jnp.concatenate([out_re, out_im], axis=0)


def tn(left, right):
    return lax.dot_general(left, right, (((0,), (0,)), ((), ())), preferred_element_type=jnp.float32)


def fused_kernel(
    volts_hbm, ids_ref, start_ref, own_ref, q_ref, left_ref,
    vol_ref, table_ref, stage, v_ref, parts_ref, pack_ref, pair_ref, half_ref, land_ref, full_ref, res_ref,
    vol_sem, own_sem, mine_sem, f_send, f_recv, z_send, z_recv,
    p_send, p_recv, k_send, k_recv, j_send, j_recv, b_send, b_recv,
    up_send, down_send, line_recv, mate_send, mate_recv,
    *, k, freq, tile,
):
    chans, _, spectra, width = parts_ref.shape
    cols = vol_ref.shape[1]
    block = spectra // tile
    rows = 2 * block
    subs = block // SUB
    window = vol_ref.shape[2]
    group = lax.axis_index("freq")
    me = lax.axis_index("tile")
    line = tile // 2
    z, core = me // 2, lax.rem(me, 2)
    mate = me + 1 - 2 * core
    barrier = pltpu.get_barrier_semaphore()
    for d in range(1, freq):
        pl.semaphore_signal(barrier, inc=1, device_id={"freq": lax.rem(group + d, freq)}, device_id_type=MESH)
    for d in range(1, tile):
        pl.semaphore_signal(barrier, inc=1, device_id={"tile": lax.rem(me + d, tile)}, device_id_type=MESH)

    def remote(src, dst, send, recv, where):
        return pltpu.make_async_remote_copy(
            src_ref=src, dst_ref=dst, send_sem=send, recv_sem=recv, device_id=where, device_id_type=MESH
        )

    def block_at(j):
        return lax.rem(j, 2) * (tile // 2) + j // 2

    def fetch(j):
        lanes = pl.ds(pl.multiple_of(block_at(j) * (block * P_SIZE), P_SIZE), window)
        return pltpu.make_async_copy(volts_hbm.at[:, lanes], vol_ref.at[j], vol_sem.at[j])

    for j in range(tile):
        fetch(j).start()

    build_table(ids_ref, table_ref)

    def rows_of(b):
        return pl.ds(pl.multiple_of(b * rows, rows), rows)

    my_cols = pl.ds(pl.multiple_of(group * cols, cols), cols)

    def handover(j, d):
        peer = lax.rem(group + d, freq)
        return remote(
            stage.at[j, peer], v_ref.at[:, rows_of(block_at(j)), my_cols],
            f_send.at[j, d - 1], f_recv.at[j, d - 1], {"freq": peer},
        )

    def own_part(j):
        return pltpu.make_async_copy(
            stage.at[j, group], v_ref.at[:, rows_of(block_at(j)), my_cols], own_sem.at[j]
        )

    def filter_step(j):
        fetch(j).wait()
        span = (SUB + TAPS - 1) * P_SIZE
        right = jnp.concatenate(
            [vol_ref[j, :, n * SUB * P_SIZE : n * SUB * P_SIZE + span] for n in range(subs)], axis=0
        )
        result = nt(table_ref[...], right)
        pieces = [result[:, n * cols : (n + 1) * cols].reshape(-1, SUB, cols) for n in range(subs)]
        result = jnp.concatenate(pieces, axis=1)
        stage[j] = result.reshape(freq, chans, rows, cols).astype(jnp.bfloat16)

    def arrive(j):
        for d in range(1, freq):
            handover(j, d).wait_recv()
        own_part(j).wait()

    def forward(j, d, b):
        f = lax.rem(group + d, freq)
        lanes = pl.ds(pl.multiple_of(f * cols, cols), cols)
        src = stage.at[j, group] if d == 0 else v_ref.at[:, rows_of(block_at(j)), lanes]
        return remote(src, own_ref.at[me, :, :, lanes], z_send.at[j, d], z_recv.at[me, f], {"tile": b})

    def keep(j, d):
        lanes = pl.ds(pl.multiple_of(lax.rem(group + d, freq) * cols, cols), cols)
        src = stage.at[j, group] if d == 0 else v_ref.at[:, rows_of(block_at(j)), lanes]
        return pltpu.make_async_copy(src, own_ref.at[me, :, :, lanes], mine_sem.at[d])

    def pass_on(j, d):
        b = block_at(j)

        @pl.when(b != me)
        def _():
            forward(j, d, b).start()

        @pl.when(b == me)
        def _():
            keep(j, d).start()

    def compute(j, carry):
        filter_step(j)
        return carry

    def dispatch(j, carry):
        for d in range(1, freq):
            handover(j, d).start()
        own_part(j).start()
        pass_on(j, 0)
        return carry

    def collect(j, carry):
        arrive(j)

        @pl.when(j < EARLY)
        def _():
            for d in range(1, freq):
                pass_on(j, d)

        return carry

    lax.fori_loop(0, tile, compute, 0)
    pl.semaphore_wait(barrier, freq - 1 + tile - 1)
    lax.fori_loop(0, tile, dispatch, 0)
    lax.fori_loop(0, tile, collect, 0)

    start = jnp.concatenate(
        [
            start_ref[:, pl.ds(pl.multiple_of(f * (tile * cols) + me * cols, cols), cols)]
            for f in range(freq)
        ],
        axis=1,
    )
    start3 = split3(start)
    fold = spectra - 128
    half = pack_ref.shape[2]
    keep_mask = lax.broadcasted_iota(jnp.int32, (spectra, spectra), 0) >= lax.broadcasted_iota(
        jnp.int32, (spectra, spectra), 1
    )
    pad_lanes = 128 - fold

    def folded(value):
        count = value.shape[0] // 2
        wide = jnp.concatenate([value[:, 128:], jnp.zeros((2 * count, pad_lanes), jnp.float32)], axis=1)
        return wide[:count] + pltpu.roll(wide[count:], fold, 1)

    def to_mate(c):
        return remote(pack_ref.at[c, 1 - core], pair_ref.at[c], p_send.at[c], p_recv.at[c], {"tile": mate})

    for c in range(chans):
        loose = v_ref[c].astype(jnp.float32).reshape(tile, 2, block, width)
        real_v = loose[:, 0].reshape(spectra, width).astype(jnp.bfloat16)
        imag_v = loose[:, 1].reshape(spectra, width).astype(jnp.bfloat16)
        parts_ref[c, 0] = real_v
        parts_ref[c, 1] = imag_v
        k_re = nt(real_v, real_v) + nt(imag_v, imag_v)
        k_im = nt(real_v, imag_v) - nt(imag_v, real_v)
        packed = jnp.where(keep_mask, k_re, k_im)
        on_re = fold3(nt(start3, real_v))
        on_im = fold3(nt(start3, imag_v))
        w = jnp.concatenate([on_re[:k] + on_im[k:], on_re[k:] - on_im[:k]], axis=0)
        tail = 2 * half - (spectra + spectra // 2 + 3 * k)
        everything = jnp.concatenate(
            [packed[:, :128], folded(packed), w[:, :128], folded(w), jnp.zeros((tail, 128), jnp.float32)], axis=0
        )
        pack_ref[c] = everything.reshape(2, half, 128)
        to_mate(c).start()

    def root_line(c):
        return line // 2 - 1 + c % 2

    def to_root(c, d):
        return remote(
            half_ref.at[c], land_ref.at[c, d - 1], k_send.at[c], k_recv.at[c, d - 1],
            {"tile": 2 * root_line(c) + core},
        )

    for c in range(chans):
        to_mate(c).wait_recv()
        half_ref[c] = pack_ref[c, core] + pair_ref[c]
        for d in range(1, line):

            @pl.when(z == (root_line(c) + d) % line)
            def _():
                to_root(c, d).start()

    for j in range(EARLY, tile):
        for d in range(1, freq):
            pass_on(j, d)

    g_re = exact(start_ref[...], start_ref[:k])
    g_im = exact(start_ref[...], start_ref[k:])
    gram0 = jnp.concatenate([g_re[:k] + g_im[k:], g_im[:k] - g_re[k:]], axis=0)

    def join(c):
        return remote(half_ref.at[c], full_ref.at[core], j_send.at[c], j_recv.at[c], {"tile": mate})

    for c in range(chans):

        @pl.when(z == root_line(c))
        def _():
            total = half_ref[c]
            for d in range(1, line):
                to_root(c, d).wait_recv()
                total = total + land_ref[c, d - 1]

            @pl.when(core == c // 2)
            def _():
                full_ref[core] = total

            @pl.when(core != c // 2)
            def _():
                half_ref[c] = total
                join(c).start()

    side = z - (line // 2 - 1)
    at = side + 2 * core
    is_root = (side >= 0) & (side < 2) & (at < chans)

    def spread(c, d):
        return remote(
            res_ref.at[c], res_ref.at[c], b_send.at[d - 1], b_recv.at[c], {"tile": lax.rem(me + d, tile)}
        )

    @pl.when(is_root)
    def _():
        for c in range(chans):

            @pl.when(at == c)
            def _():
                join(c).wait_recv()

        res_ref[at] = iterate(full_ref[...].reshape(2 * half, 128), gram0, k, spectra)
        for d in range(1, tile):
            spread(at, d).start()

    def line_copy(c, origin, to, sem):
        slot = 2 * origin + core
        return remote(
            q_ref.at[slot, c], q_ref.at[slot, c], sem.at[c, origin], line_recv.at[c, origin], {"tile": 2 * to + core}
        )

    def mate_copy(c, origin):
        slot = 2 * origin + core
        return remote(
            q_ref.at[slot, c], q_ref.at[slot, c], mate_send.at[c, origin], mate_recv.at[c, origin], {"tile": mate}
        )

    def send_on(c, origin, up, down):
        if up:

            @pl.when(z < line - 1)
            def _():
                line_copy(c, origin, z + 1, up_send).start()

        if down:

            @pl.when(z > 0)
            def _():
                line_copy(c, origin, z - 1, down_send).start()

        mate_copy(c, origin).start()

    for c in range(chans):

        @pl.when(jnp.logical_not(is_root & (at == c)))
        def _():
            spread(c, 1).wait_recv()

        w = res_ref[c, :, :spectra]
        a = res_ref[c, :, 256 : 256 + spectra]
        b = res_ref[c, :, 512:640]
        parts = split3(a)
        on_re = fold3(plain(parts, parts_ref[c, 0]))
        on_im = fold3(plain(parts, parts_ref[c, 1]))
        q = jnp.concatenate([on_re[:k] - on_im[k:], on_re[k:] + on_im[:k]], axis=0)
        q_ref[me, c] = q + mix(b[:k], b[k:], start, k)
        send_on(c, z, True, True)
        turned = jnp.concatenate([-w[k:], w[:k]], axis=0)
        chosen = jnp.zeros((2 * k, rows), jnp.float32)
        for t in range(tile):
            lanes = slice(t * block, (t + 1) * block)
            pair = jnp.concatenate([w[:, lanes], turned[:, lanes]], axis=1)
            chosen = jnp.where(me == t, pair, chosen)
        left_ref[c] = chosen

    for d in range(1, line):
        for c in range(chans):

            @pl.when(z >= d)
            def _():
                line_copy(c, z - d, z, up_send).wait_recv()
                send_on(c, z - d, True, False)

            @pl.when(z + d < line)
            def _():
                line_copy(c, z + d, z, down_send).wait_recv()
                send_on(c, z + d, False, True)

    for c in range(chans):
        for origin in range(line):
            mate_copy(c, origin).wait()

            @pl.when((z >= origin) & (z < line - 1))
            def _():
                line_copy(c, origin, z + 1, up_send).wait_send()

            @pl.when((z <= origin) & (z > 0))
            def _():
                line_copy(c, origin, z - 1, down_send).wait_send()

    def drain(j, carry):
        for d in range(1, freq):
            handover(j, d).wait_send()

        b = block_at(j)

        @pl.when(b != me)
        def _():
            for d in range(freq):
                forward(j, d, b).wait_send()
                lanes = pl.ds(d * cols, cols)
                piece = own_ref.at[b, :, :, lanes]
                remote(piece, piece, z_send.at[j, d], z_recv.at[b, d], {"tile": b}).wait_recv()

        @pl.when(b == me)
        def _():
            for d in range(freq):
                keep(j, d).wait()

        return carry

    lax.fori_loop(0, tile, drain, 0)
    for c in range(chans):
        to_mate(c).wait_send()

        @pl.when(z != root_line(c))
        def _():
            to_root(c, 1).wait_send()

        @pl.when((z == root_line(c)) & (core != c // 2))
        def _():
            join(c).wait_send()

    @pl.when(is_root)
    def _():
        for d in range(1, tile):
            spread(at, d).wait_send()


def exact(left, right):
    return lax.dot_general(
        left, right, (((1,), (1,)), ((), ())), precision=highest, preferred_element_type=jnp.float32
    )


def build_table(ids_ref, table_ref):
    channels = ids_ref.shape[0]
    count = 2 * channels
    length = TAPS * P_SIZE
    tap = lax.broadcasted_iota(jnp.int32, (8, P_SIZE), 0)
    point = lax.broadcasted_iota(jnp.int32, (8, P_SIZE), 1)
    offsets = (tap * P_SIZE + point).astype(jnp.float32)
    shifted = math.pi * ((offsets + 0.5 - length / 2.0) / P_SIZE)
    shape = jnp.sin(shifted) / shifted
    shape = shape * (0.5 - 0.5 * jnp.cos(2.0 * math.pi * (offsets + 0.5) / length))
    shape = jnp.where(tap < TAPS, shape, 0.0)
    total = jnp.sum(jnp.sum(shape * shape, axis=1, keepdims=True), axis=0, keepdims=True)
    shape = shape / jnp.sqrt(total)
    part = lax.broadcasted_iota(jnp.int32, (count, P_SIZE), 0)
    place = lax.broadcasted_iota(jnp.int32, (count, P_SIZE), 1)
    ids = jnp.zeros((count, P_SIZE), jnp.int32)
    for c in range(channels):
        ids = jnp.where(part // 2 == c, ids_ref[c], ids)
    phases = jnp.bitwise_and(ids * place, P_SIZE - 1)
    angles = 2.0 * math.pi / P_SIZE * phases.astype(jnp.float32)
    rotors = jnp.where(jnp.bitwise_and(part, 1) == 0, jnp.cos(angles), -jnp.sin(angles))
    spread = []
    for m in range(TAPS):
        taps = rotors * shape[m : m + 1]
        spread.append(jnp.broadcast_to(taps[:, None, :], (count, SUB, P_SIZE)))
    at = lax.broadcasted_iota(jnp.int32, (count, SUB, P_SIZE), 1)
    for frame in range(SUB + TAPS - 1):
        value = jnp.zeros((count, SUB, P_SIZE), jnp.float32)
        for m in range(TAPS):
            if 0 <= frame - m < SUB:
                value = jnp.where(at == frame - m, spread[m], value)
        table_ref[:, frame * P_SIZE : (frame + 1) * P_SIZE] = value.reshape(count * SUB, P_SIZE).astype(jnp.bfloat16)


def iterate(full, gram0, k, spectra):
    fold = spectra - 128
    count = spectra // 2
    lane = lax.broadcasted_iota(jnp.int32, (1, 128), 1)

    def unfold(top, bent):
        low = jnp.where(lane < fold, bent, 0.0)
        high = jnp.where(lane < fold, pltpu.roll(bent, 128 - fold, 1), 0.0)
        return jnp.concatenate([top, jnp.concatenate([low, high], axis=0)], axis=1)

    packed = unfold(full[:spectra], full[spectra : spectra + count])
    at = spectra + count
    w = unfold(full[at : at + 2 * k], full[at + 2 * k : at + 3 * k])
    packed = jnp.concatenate([packed, jnp.zeros((256 - spectra, 256), jnp.float32)], axis=0)
    turned = packed.T
    row = lax.broadcasted_iota(jnp.int32, (256, 256), 0)
    col = lax.broadcasted_iota(jnp.int32, (256, 256), 1)
    k_re = jnp.where(row >= col, packed, turned)
    k_im = jnp.where(row < col, packed, jnp.where(row > col, -turned, 0.0))
    both = jnp.concatenate([k_re, k_im], axis=1)
    high = both.astype(jnp.bfloat16)
    rest = both - high.astype(jnp.float32)
    mid = rest.astype(jnp.bfloat16)
    low = (rest - mid.astype(jnp.float32)).astype(jnp.bfloat16)
    n2 = 2 * k
    a = jnp.zeros((n2, 256), jnp.float32)
    b = jnp.where(
        lax.broadcasted_iota(jnp.int32, (n2, 128), 0) == lax.broadcasted_iota(jnp.int32, (n2, 128), 1), 1.0, 0.0
    )
    b = jnp.where(lax.broadcasted_iota(jnp.int32, (n2, 128), 0) < k, b, 0.0)
    held = gram0
    for _ in range(ITERS):
        w3 = split3(w)
        on_high = plain(w3, high)
        on_mid = plain(w3[: 2 * n2], mid)
        on_low = plain(w3[:n2], low)
        kw = (on_low + on_mid[n2:] + on_high[2 * n2 :]) + (on_mid[:n2] + on_high[n2 : 2 * n2]) + on_high[:n2]
        on_re, on_im = kw[:, :256], kw[:, 256:]
        kw = jnp.concatenate([on_re[:k] + on_im[k:], on_re[k:] - on_im[:k]], axis=0)
        y = kw / spectra + loading * w
        u = (y + loading * w) / spectra
        g_re = exact(w, u[:k])
        g_im = exact(w, u[k:])
        gram = jnp.concatenate([g_re[:k] + g_im[k:], g_im[:k] - g_re[k:]], axis=0) + loading * loading * held
        m_re, m_im = inverse_factor(gram, k)
        grown = jnp.concatenate([y, w / spectra + loading * a, loading * b], axis=1)
        grown = mix(m_re, m_im, grown, k)
        w, a, b = grown[:, :256], grown[:, 256:512], grown[:, 512:]
        held = b_identity(n2, k)
    return jnp.concatenate([w, a, b], axis=1)


def b_identity(n2, k):
    row = lax.broadcasted_iota(jnp.int32, (n2, k), 0)
    col = lax.broadcasted_iota(jnp.int32, (n2, k), 1)
    return jnp.where(row == col, 1.0, 0.0)


def finish_kernel(own_ref, q_ref, left_ref, out_ref):
    tile, chans, rows, cols = own_ref.shape
    block = rows // 2
    n2 = q_ref.shape[2]
    for c in range(chans):
        w3 = split3(left_ref[c])
        w_left = jnp.concatenate([w3[:n2], w3[:n2], w3[n2 : 2 * n2], w3[n2 : 2 * n2], w3[:n2], w3[2 * n2 :]], axis=0)
        for t in range(tile):
            s3 = split3(q_ref[t, c])
            s_right = jnp.concatenate(
                [s3[:n2], s3[n2 : 2 * n2], s3[:n2], s3[n2 : 2 * n2], s3[2 * n2 :], s3[:n2]], axis=0
            )
            cleaned = own_ref[t, c].astype(jnp.float32) - tn(w_left, s_right)
            out_ref[0, c, :, t * cols : (t + 1) * cols] = cleaned[:block]
            out_ref[1, c, :, t * cols : (t + 1) * cols] = cleaned[block:]


def channelize_kernel(volts_ref, table_ref, out_ref):
    step = pl.program_id(0)
    span = (STEP + TAPS - 1) * P_SIZE
    start = pl.multiple_of(step * (STEP * P_SIZE), P_SIZE)
    chunk = volts_ref[:, pl.ds(start, span)]
    result = nt(table_ref[...], chunk)
    out_ref[...] = result.reshape(out_ref.shape).astype(jnp.bfloat16)


def channelize(voltages, table, rows, spectra_all):
    inputs_local, samples = voltages.shape
    return pl.pallas_call(
        channelize_kernel,
        grid=(spectra_all // STEP,),
        in_specs=[VMEM, VMEM],
        out_specs=pl.BlockSpec((rows, STEP, inputs_local), lambda i: (0, i, 0)),
        out_shape=jax.ShapeDtypeStruct((rows, spectra_all, inputs_local), jnp.bfloat16),
        compiler_params=pltpu.CompilerParams(vmem_limit_bytes=40 * 2**20),
    )(voltages, table)


def start_kernel(v_ref, q_ref, pg_ref, *, k, lanes):
    chans, _, spectra, _ = v_ref.shape
    pg_ref[...] = jnp.zeros_like(pg_ref)
    for c in range(chans):
        pg_ref[2 * k * c : 2 * k * (c + 1), :spectra] = project(q_ref[...], v_ref[c, 0], v_ref[c, 1], k)


def step_kernel(v_ref, z_ref, pg_ref, z_out, pg_out, *, k, lanes, first):
    chans, _, spectra, width = v_ref.shape
    pg_out[...] = jnp.zeros_like(pg_out)
    for c in range(chans):
        at = slice(2 * k * c, 2 * k * (c + 1))
        weights = pg_ref[at, :spectra]
        basis = z_ref[...] if first else z_ref[c]
        if not first:
            m_re, m_im = inverse_factor(pg_ref[at, lanes:], k)
            weights = mix(m_re, m_im, weights, k)
            basis = mix(m_re, m_im, basis, k)
        real_v, imag_v = v_ref[c, 0], v_ref[c, 1]
        parts = split3(weights / spectra)
        on_re = fold3(plain(parts, real_v))
        on_im = fold3(plain(parts, imag_v))
        z = jnp.concatenate([on_re[:k] - on_im[k:], on_re[k:] + on_im[:k]], axis=0) + loading * basis
        z_out[c] = z
        pg_out[at, :spectra] = project(z, real_v, imag_v, k)
        pad = jnp.zeros((lanes_pad(k), width), jnp.float32)
        right = jnp.concatenate([z[:k], pad], axis=0)
        right_im = jnp.concatenate([z[k:], pad], axis=0)
        dims = (((1,), (1,)), ((), ()))
        first_dot = lax.dot_general(z, right, dims, precision=highest, preferred_element_type=jnp.float32)
        second_dot = lax.dot_general(z, right_im, dims, precision=highest, preferred_element_type=jnp.float32)
        g_re = first_dot[:k] + second_dot[k:]
        g_im = second_dot[:k] - first_dot[k:]
        pg_out[at, lanes:] = jnp.concatenate([g_re, g_im], axis=0)


def lanes_pad(k):
    return 128 - k


def clean_kernel(v_ref, z_ref, pg_ref, out_ref, *, k, lanes):
    chans, _, spectra, width = v_ref.shape
    parts_count, _, _, block, _ = out_ref.shape
    for c in range(chans):
        at = slice(2 * k * c, 2 * k * (c + 1))
        m_re, m_im = inverse_factor(pg_ref[at, lanes:], k)
        w = mix(m_re, m_im, pg_ref[at, :spectra], k)
        q = mix(m_re, m_im, z_ref[c], k)
        turned = jnp.concatenate([q[k:], -q[:k]], axis=0)
        w3 = split3(w)
        n2 = 2 * k
        w_left = jnp.concatenate([w3[:n2], w3[:n2], w3[n2 : 2 * n2], w3[n2 : 2 * n2], w3[:n2], w3[2 * n2 :]], axis=0)
        for r, side in ((0, q), (1, turned)):
            s3 = split3(side)
            s_right = jnp.concatenate(
                [s3[:n2], s3[n2 : 2 * n2], s3[:n2], s3[n2 : 2 * n2], s3[2 * n2 :], s3[:n2]], axis=0
            )
            fitted = tn(w_left, s_right)
            cleaned = v_ref[c, r].astype(jnp.float32) - fitted
            out_ref[:, r, c] = cleaned.reshape(parts_count, block, width).astype(jnp.bfloat16)


def reduce_kernel(x_ref, out_ref, land_ref, send1, recv1, send2, recv2, *, size, chunk):
    me = lax.axis_index("tile")
    barrier = pltpu.get_barrier_semaphore()
    for d in range(1, size):
        peer = lax.rem(me + d, size)
        pl.semaphore_signal(barrier, inc=1, device_id={"tile": peer}, device_id_type=MESH)
    pl.semaphore_wait(barrier, size - 1)
    mine = pl.ds(pl.multiple_of(me * chunk, 8), chunk)
    sends = []
    for d in range(1, size):
        peer = lax.rem(me + d, size)
        copy = pltpu.make_async_remote_copy(
            src_ref=x_ref.at[pl.ds(pl.multiple_of(peer * chunk, 8), chunk)],
            dst_ref=land_ref.at[d - 1],
            send_sem=send1.at[d - 1],
            recv_sem=recv1.at[d - 1],
            device_id={"tile": peer},
            device_id_type=MESH,
        )
        copy.start()
        sends.append(copy)
    total = x_ref[mine]
    for d in range(1, size):
        sends[d - 1].wait_recv()
        total = total + land_ref[d - 1]
    out_ref[mine] = total
    later = []
    for d in range(1, size):
        peer = lax.rem(me + d, size)
        copy = pltpu.make_async_remote_copy(
            src_ref=out_ref.at[mine],
            dst_ref=out_ref.at[mine],
            send_sem=send2.at[d - 1],
            recv_sem=recv2.at[d - 1],
            device_id={"tile": peer},
            device_id_type=MESH,
        )
        copy.start()
        later.append(copy)
    for copy in later:
        copy.wait_recv()
    for copy in sends + later:
        copy.wait_send()


def tile_sum(x, size):
    rows, width = x.shape
    chunk = rows // size
    return pl.pallas_call(
        functools.partial(reduce_kernel, size=size, chunk=chunk),
        in_specs=[VMEM],
        out_specs=VMEM,
        out_shape=jax.ShapeDtypeStruct(x.shape, jnp.float32),
        scratch_shapes=[pltpu.VMEM((size - 1, chunk, width), jnp.float32)]
        + [pltpu.SemaphoreType.DMA((size - 1,))] * 4,
        compiler_params=pltpu.CompilerParams(collective_id=0, has_side_effects=True),
    )(x)


def up(value, unit):
    return -(-value // unit) * unit


def body_split(voltages, channel_ids, start_basis):
    inputs_local, samples_count = voltages.shape
    freq_count = lax.axis_size("freq")
    tile_count = lax.axis_size("tile")
    channels = channel_ids.shape[0]
    chan_local = channels // freq_count
    spectra_all = samples_count // P_SIZE - TAPS + 1
    spectra_local = spectra_all // tile_count
    k = start_basis.shape[1]
    width = freq_count * inputs_local

    coeffs = make_table(channel_ids, TAPS, P_SIZE).reshape(TAPS, 2 * channels, P_SIZE)
    local = channelize(voltages, banded(coeffs), 2 * channels, spectra_all)
    parcel = local.reshape(2, freq_count, chan_local, spectra_all, inputs_local)
    arrived = lax.all_to_all(parcel, "freq", split_axis=1, concat_axis=1, tiled=True)
    values = jnp.transpose(arrived, (2, 0, 3, 1, 4)).reshape(chan_local, 2, spectra_all, width)

    mine = lax.axis_index("tile")
    start = start_basis.reshape(2 * k, freq_count, tile_count, inputs_local)
    start = lax.dynamic_index_in_dim(start, mine, 2, keepdims=False).reshape(2 * k, width)

    lanes = up(spectra_all, 128)
    chunk = up(-(-chan_local * 2 * k // tile_count), 8)
    packed = jax.ShapeDtypeStruct((tile_count * chunk, lanes + 128), jnp.float32)
    z_shape = jax.ShapeDtypeStruct((chan_local, 2 * k, width), jnp.float32)
    params = pltpu.CompilerParams(vmem_limit_bytes=40 * 2**20)

    partial = pl.pallas_call(
        functools.partial(start_kernel, k=k, lanes=lanes),
        in_specs=[VMEM] * 2, out_specs=VMEM, out_shape=packed, compiler_params=params,
    )(values, start)
    z = start
    for step_at in range(ITERS):
        total = tile_sum(partial, tile_count)
        z, partial = pl.pallas_call(
            functools.partial(step_kernel, k=k, lanes=lanes, first=step_at == 0),
            in_specs=[VMEM] * 3, out_specs=[VMEM] * 2, out_shape=[z_shape, packed],
            compiler_params=params,
        )(values, z, total)
    total = tile_sum(partial, tile_count)
    cleaned = pl.pallas_call(
        functools.partial(clean_kernel, k=k, lanes=lanes),
        in_specs=[VMEM] * 3, out_specs=VMEM,
        out_shape=jax.ShapeDtypeStruct((tile_count, 2, chan_local, spectra_local, width), jnp.bfloat16),
        compiler_params=params,
    )(values, z, total)
    moved = lax.all_to_all(cleaned, "tile", split_axis=0, concat_axis=0, tiled=True)
    moved = moved.reshape(tile_count, 2, chan_local, spectra_local, freq_count, inputs_local)
    moved = jnp.transpose(moved, (1, 2, 3, 4, 0, 5)).astype(jnp.float32)
    return moved.reshape(2, chan_local, spectra_local, freq_count * tile_count * inputs_local)


def body(voltages, channel_ids, start_basis):
    inputs_local, samples_count = voltages.shape
    freq_count = lax.axis_size("freq")
    tile_count = lax.axis_size("tile")
    if inputs_local % 128:
        return body_split(voltages, channel_ids, start_basis)
    channels = channel_ids.shape[0]
    chan_local = channels // freq_count
    spectra_all = samples_count // P_SIZE - TAPS + 1
    spectra_local = spectra_all // tile_count
    k = start_basis.shape[1]
    width = freq_count * inputs_local
    if spectra_all != 192 or spectra_local % SUB or tile_count % 4 or chan_local > 4 or k != 8:
        return body_split(voltages, channel_ids, start_basis)

    start = start_basis.reshape(2 * k, freq_count * tile_count * inputs_local)
    rows = 2 * spectra_local
    line = tile_count // 2
    half = up(spectra_all + spectra_all // 2 + 3 * k, 16) // 2
    sem = pltpu.SemaphoreType.DMA
    peers = freq_count - 1
    own, q, left = pl.pallas_call(
        functools.partial(fused_kernel, k=k, freq=freq_count, tile=tile_count),
        in_specs=[pl.BlockSpec(memory_space=pl.ANY), pl.BlockSpec(memory_space=pltpu.SMEM), VMEM],
        out_specs=[pl.BlockSpec(memory_space=pl.ANY), VMEM, VMEM],
        out_shape=[
            jax.ShapeDtypeStruct((tile_count, chan_local, rows, width), jnp.bfloat16),
            jax.ShapeDtypeStruct((tile_count, chan_local, 2 * k, width), jnp.float32),
            jax.ShapeDtypeStruct((chan_local, 2 * k, rows), jnp.float32),
        ],
        scratch_shapes=[
            pltpu.VMEM((tile_count, inputs_local, (spectra_local + TAPS - 1) * P_SIZE), jnp.bfloat16),
            pltpu.VMEM((2 * channels * SUB, (SUB + TAPS - 1) * P_SIZE), jnp.bfloat16),
            pltpu.VMEM((tile_count, freq_count, chan_local, rows, inputs_local), jnp.bfloat16),
            pltpu.VMEM((chan_local, tile_count * rows, width), jnp.bfloat16),
            pltpu.VMEM((chan_local, 2, spectra_all, width), jnp.bfloat16),
            pltpu.VMEM((chan_local, 2, half, 128), jnp.float32),
            pltpu.VMEM((chan_local, half, 128), jnp.float32),
            pltpu.VMEM((chan_local, half, 128), jnp.float32),
            pltpu.VMEM((chan_local, line - 1, half, 128), jnp.float32),
            pltpu.VMEM((2, half, 128), jnp.float32),
            pltpu.VMEM((chan_local, 2 * k, 640), jnp.float32),
            sem((tile_count,)), sem((tile_count,)), sem((freq_count,)),
            sem((tile_count, peers)), sem((tile_count, peers)),
            sem((tile_count, freq_count)), sem((tile_count, freq_count)),
            sem((chan_local,)), sem((chan_local,)),
            sem((chan_local,)), sem((chan_local, line - 1)),
            sem((chan_local,)), sem((chan_local,)),
            sem((tile_count - 1,)), sem((chan_local,)),
            sem((chan_local, line)), sem((chan_local, line)), sem((chan_local, line)),
            sem((chan_local, line)), sem((chan_local, line)),
        ],
        compiler_params=pltpu.CompilerParams(
            collective_id=0, has_side_effects=True, vmem_limit_bytes=56 * 2**20
        ),
    )(voltages, channel_ids, start)
    stride = tile_count * inputs_local
    return pl.pallas_call(
        finish_kernel,
        grid=(freq_count,),
        in_specs=[
            pl.BlockSpec((tile_count, chan_local, rows, inputs_local), lambda f: (0, 0, 0, f)),
            pl.BlockSpec((tile_count, chan_local, 2 * k, inputs_local), lambda f: (0, 0, 0, f)),
            pl.BlockSpec((chan_local, 2 * k, rows), lambda f: (0, 0, 0)),
        ],
        out_specs=pl.BlockSpec((2, chan_local, spectra_local, stride), lambda f: (0, 0, 0, f)),
        out_shape=jax.ShapeDtypeStruct((2, chan_local, spectra_local, freq_count * stride), jnp.float32),
        compiler_params=pltpu.CompilerParams(vmem_limit_bytes=60 * 2**20),
    )(own, q, left)


def solution(mesh):
    in_specs = (P(("freq", "tile"), None), P(), P())
    out_specs = P(None, "freq", "tile", None)
    return jax.shard_map(body, mesh=mesh, in_specs=in_specs, out_specs=out_specs, check_vma=False)
```

```python
import functools
import math

import jax
import jax.numpy as jnp
from jax import lax
from jax.experimental import pallas as pl
from jax.experimental.pallas import tpu as pltpu
from jax.sharding import PartitionSpec as P

TAPS = 4
P_SIZE = 128
ITERS = 3
STEP = 16
SUB = 8
EARLY = 4
AHEAD = 5

loading = 0.5
highest = lax.Precision.HIGHEST
VMEM = pl.BlockSpec(memory_space=pltpu.VMEM)
MESH = pl.DeviceIdType.MESH


def make_table(channel_ids, taps_count, points):
    length = taps_count * points
    offsets = jnp.arange(length, dtype=jnp.float32)
    shifted = (offsets + 0.5 - length / 2.0) / points
    window = jnp.sinc(shifted) * (0.5 - 0.5 * jnp.cos(2.0 * math.pi * (offsets + 0.5) / length))
    window = window / jnp.sqrt(jnp.sum(window * window))
    window = window.reshape(taps_count, points)
    phases = channel_ids[:, None] * jnp.arange(points, dtype=jnp.int32)[None, :] % points
    angles = 2.0 * math.pi / points * phases.astype(jnp.float32)
    rotors = jnp.stack([jnp.cos(angles), -jnp.sin(angles)])
    return (window[:, None, None, :] * rotors[None]).astype(jnp.bfloat16)


def banded(coeffs):
    rows = coeffs.shape[1]
    spect = lax.broadcasted_iota(jnp.int32, (1, STEP, STEP + TAPS - 1, 1), 1)
    frame = lax.broadcasted_iota(jnp.int32, (1, STEP, STEP + TAPS - 1, 1), 2)
    table = jnp.zeros((rows, STEP, STEP + TAPS - 1, P_SIZE), jnp.bfloat16)
    for tap in range(TAPS):
        table = jnp.where(frame - spect == tap, coeffs[tap][:, None, None, :], table)
    return table.reshape(rows * STEP, (STEP + TAPS - 1) * P_SIZE)


def nt(left, right):
    return lax.dot_general(left, right, (((1,), (1,)), ((), ())), preferred_element_type=jnp.float32)


def split3(value):
    high = value.astype(jnp.bfloat16)
    rest = value - high.astype(jnp.float32)
    mid = rest.astype(jnp.bfloat16)
    low = (rest - mid.astype(jnp.float32)).astype(jnp.bfloat16)
    return jnp.concatenate([high, mid, low], axis=0)


def fold3(value):
    rows = value.shape[0] // 3
    return value[:rows] + value[rows : 2 * rows] + value[2 * rows :]


def plain(left, right):
    return lax.dot_general(left, right, (((1,), (0,)), ((), ())), preferred_element_type=jnp.float32)


def project(z, real_v, imag_v, k):
    parts = split3(z)
    on_re = fold3(nt(parts, real_v))
    on_im = fold3(nt(parts, imag_v))
    return jnp.concatenate([on_re[:k] + on_im[k:], on_re[k:] - on_im[:k]], axis=0)


def inverse_factor(gram, k, off=0):
    lanes = gram.shape[1]
    col = lax.broadcasted_iota(jnp.int32, (k, lanes), 1)
    row = lax.broadcasted_iota(jnp.int32, (k, lanes), 0)
    zero = jnp.zeros((k, lanes), jnp.float32)
    a_re = gram[:k]
    a_im = gram[k:]
    m_re = jnp.where(col == row, 1.0, zero)
    m_im = zero
    for j in range(k):
        at_col = col == j + off
        c_re = jnp.sum(jnp.where(at_col, a_re, 0.0), axis=1, keepdims=True)
        c_im = jnp.sum(jnp.where(at_col, a_im, 0.0), axis=1, keepdims=True)
        pivot = jnp.sqrt(c_re[j : j + 1])
        l_re = jnp.where(row[:, :1] > j, c_re / pivot, 0.0)
        l_im = jnp.where(row[:, :1] > j, c_im / pivot, 0.0)
        ar, ai = a_re[j : j + 1] / pivot, a_im[j : j + 1] / pivot
        mr, mi = m_re[j : j + 1] / pivot, m_im[j : j + 1] / pivot
        here = row == j
        a_re = jnp.where(here, ar, a_re - (l_re * ar - l_im * ai))
        a_im = jnp.where(here, ai, a_im - (l_re * ai + l_im * ar))
        m_re = jnp.where(here, mr, m_re - (l_re * mr - l_im * mi))
        m_im = jnp.where(here, mi, m_im - (l_re * mi + l_im * mr))
    return m_re, -m_im


def mix(m_re, m_im, rows, k):
    out_re = jnp.zeros((k, rows.shape[1]), jnp.float32)
    out_im = jnp.zeros((k, rows.shape[1]), jnp.float32)
    for j in range(k):
        f_re, f_im = m_re[:, j : j + 1], m_im[:, j : j + 1]
        r_re, r_im = rows[j : j + 1], rows[k + j : k + j + 1]
        out_re = out_re + (f_re * r_re - f_im * r_im)
        out_im = out_im + (f_re * r_im + f_im * r_re)
    return jnp.concatenate([out_re, out_im], axis=0)


def tn(left, right):
    return lax.dot_general(left, right, (((0,), (0,)), ((), ())), preferred_element_type=jnp.float32)


def fused_kernel(
    volts_hbm, ids_ref, start_ref, own_ref, q_ref, left_ref,
    vol_ref, table_ref, stage, v_ref, parts_ref, pack_ref, pair_ref, half_ref, land_ref, full_ref, res_ref,
    vol_sem, own_sem, mine_sem, f_send, f_recv, z_send, z_recv,
    p_send, p_recv, k_send, k_recv, j_send, j_recv, b_send, b_recv,
    line_send, line_recv, mate_send, mate_recv,
    *, k, freq, tile,
):
    chans, _, spectra, width = parts_ref.shape
    cols = vol_ref.shape[1]
    block = spectra // tile
    rows = 2 * block
    subs = block // SUB
    window = vol_ref.shape[2]
    group = lax.axis_index("freq")
    me = lax.axis_index("tile")
    line = tile // 2
    z, core = me // 2, lax.rem(me, 2)
    mate = me + 1 - 2 * core
    barrier = pltpu.get_barrier_semaphore()
    for d in range(1, freq):
        pl.semaphore_signal(barrier, inc=1, device_id={"freq": lax.rem(group + d, freq)}, device_id_type=MESH)
    for d in range(1, tile):
        pl.semaphore_signal(barrier, inc=1, device_id={"tile": lax.rem(me + d, tile)}, device_id_type=MESH)

    def remote(src, dst, send, recv, where):
        return pltpu.make_async_remote_copy(
            src_ref=src, dst_ref=dst, send_sem=send, recv_sem=recv, device_id=where, device_id_type=MESH
        )

    def block_at(j):
        return lax.rem(j, 2) * (tile // 2) + j // 2

    def fetch(j):
        lanes = pl.ds(pl.multiple_of(block_at(j) * (block * P_SIZE), P_SIZE), window)
        return pltpu.make_async_copy(volts_hbm.at[:, lanes], vol_ref.at[j], vol_sem.at[j])

    for j in range(tile):
        fetch(j).start()

    build_table(ids_ref, table_ref)

    def handover(j, d):
        peer = lax.rem(group + d, freq)
        return remote(
            stage.at[j, peer], v_ref.at[j, group],
            f_send.at[j, d - 1], f_recv.at[j, d - 1], {"freq": peer},
        )

    def own_part(j):
        return pltpu.make_async_copy(stage.at[j, group], v_ref.at[j, group], own_sem.at[j])

    def filter_step(j):
        fetch(j).wait()
        span = (SUB + TAPS - 1) * P_SIZE
        right = jnp.concatenate(
            [vol_ref[j, :, n * SUB * P_SIZE : n * SUB * P_SIZE + span] for n in range(subs)], axis=0
        )
        result = nt(table_ref[...], right)
        pieces = [result[:, n * cols : (n + 1) * cols].reshape(-1, SUB, cols) for n in range(subs)]
        result = jnp.concatenate(pieces, axis=1)
        stage[j] = result.reshape(freq, chans, rows, cols).astype(jnp.bfloat16)

    def arrive(j):
        for d in range(1, freq):
            handover(j, d).wait_recv()
        own_part(j).wait()

    def forward(j, d, b):
        f = lax.rem(group + d, freq)
        src = stage.at[j, group] if d == 0 else v_ref.at[j, f]
        return remote(src, own_ref.at[me, f], z_send.at[j, d], z_recv.at[me, f], {"tile": b})

    def keep(j, d):
        f = lax.rem(group + d, freq)
        src = stage.at[j, group] if d == 0 else v_ref.at[j, f]
        return pltpu.make_async_copy(src, own_ref.at[me, f], mine_sem.at[d])

    def pass_on(j, d):
        b = block_at(j)

        @pl.when(b != me)
        def _():
            forward(j, d, b).start()

        @pl.when(b == me)
        def _():
            keep(j, d).start()

    def compute(j, carry):
        filter_step(j)
        return carry

    def dispatch(j, carry):
        for d in range(1, freq):
            handover(j, d).start()
        own_part(j).start()
        pass_on(j, 0)
        return carry

    def collect(j, carry):
        arrive(j)

        @pl.when(j < EARLY)
        def _():
            for d in range(1, freq):
                pass_on(j, d)

        return carry

    def pace(j, carry):
        filter_step(j)
        return dispatch(j, carry)

    lax.fori_loop(0, AHEAD, compute, 0)
    pl.semaphore_wait(barrier, freq - 1 + tile - 1)
    lax.fori_loop(0, AHEAD, dispatch, 0)
    lax.fori_loop(AHEAD, tile, pace, 0)
    lax.fori_loop(0, tile, collect, 0)

    start = jnp.concatenate(
        [
            start_ref[:, pl.ds(pl.multiple_of(f * (tile * cols) + me * cols, cols), cols)]
            for f in range(freq)
        ],
        axis=1,
    )
    start3 = split3(start)
    fold = spectra - 128
    half = pack_ref.shape[2]
    keep_mask = lax.broadcasted_iota(jnp.int32, (spectra, spectra), 0) >= lax.broadcasted_iota(
        jnp.int32, (spectra, spectra), 1
    )
    pad_lanes = 128 - fold

    def folded(value):
        count = value.shape[0] // 2
        wide = jnp.concatenate([value[:, 128:], jnp.zeros((2 * count, pad_lanes), jnp.float32)], axis=1)
        return wide[:count] + pltpu.roll(wide[count:], fold, 1)

    def to_mate(c):
        return remote(pack_ref.at[c, 1 - core], pair_ref.at[c], p_send.at[c], p_recv.at[c], {"tile": mate})

    for c in range(chans):
        loose = [v_ref[:, f, c].astype(jnp.float32).reshape(tile, 2, block, cols) for f in range(freq)]
        real_v, imag_v = [
            jnp.concatenate([part[:, r].reshape(spectra, cols) for part in loose], axis=1).astype(jnp.bfloat16)
            for r in range(2)
        ]
        parts_ref[c, 0] = real_v
        parts_ref[c, 1] = imag_v
        k_re = nt(real_v, real_v) + nt(imag_v, imag_v)
        k_im = nt(real_v, imag_v) - nt(imag_v, real_v)
        packed = jnp.where(keep_mask, k_re, k_im)
        on_re = fold3(nt(start3, real_v))
        on_im = fold3(nt(start3, imag_v))
        w = jnp.concatenate([on_re[:k] + on_im[k:], on_re[k:] - on_im[:k]], axis=0)
        tail = 2 * half - (spectra + spectra // 2 + 3 * k)
        everything = jnp.concatenate(
            [packed[:, :128], folded(packed), w[:, :128], folded(w), jnp.zeros((tail, 128), jnp.float32)], axis=0
        )
        pack_ref[c] = everything.reshape(2, half, 128)
        to_mate(c).start()

    def root_line(c):
        return line // 2 - 1 + c % 2

    def to_root(c, d):
        return remote(
            half_ref.at[c], land_ref.at[c, d - 1], k_send.at[c], k_recv.at[c, d - 1],
            {"tile": 2 * root_line(c) + core},
        )

    for c in range(chans):
        to_mate(c).wait_recv()
        half_ref[c] = pack_ref[c, core] + pair_ref[c]
        for d in range(1, line):

            @pl.when(z == (root_line(c) + d) % line)
            def _():
                to_root(c, d).start()

    for j in range(EARLY, tile):
        for d in range(1, freq):
            pass_on(j, d)

    g_re = exact(start_ref[...], start_ref[:k])
    g_im = exact(start_ref[...], start_ref[k:])
    gram0 = jnp.concatenate([g_re[:k] + g_im[k:], g_im[:k] - g_re[k:]], axis=0)

    def join(c):
        return remote(half_ref.at[c], full_ref.at[core], j_send.at[c], j_recv.at[c], {"tile": mate})

    for c in range(chans):

        @pl.when(z == root_line(c))
        def _():
            total = half_ref[c]
            for d in range(1, line):
                to_root(c, d).wait_recv()
                total = total + land_ref[c, d - 1]

            @pl.when(core == c // 2)
            def _():
                full_ref[core] = total

            @pl.when(core != c // 2)
            def _():
                half_ref[c] = total
                join(c).start()

    side = z - (line // 2 - 1)
    at = side + 2 * core
    is_root = (side >= 0) & (side < 2) & (at < chans)

    def spread(c, d):
        return remote(
            res_ref.at[c], res_ref.at[c], b_send.at[d - 1], b_recv.at[c], {"tile": lax.rem(me + d, tile)}
        )

    @pl.when(is_root)
    def _():
        for c in range(chans):

            @pl.when(at == c)
            def _():
                join(c).wait_recv()

        res_ref[at] = iterate(full_ref[...].reshape(2 * half, 128), gram0, k, spectra)
        for d in range(1, tile):
            spread(at, d).start()

    def line_copy(c, d):
        return remote(
            q_ref.at[me, c], q_ref.at[me, c], line_send.at[c, d - 1], line_recv.at[c, z],
            {"tile": lax.rem(me + 2 * d, tile)},
        )

    def line_arrival(c, origin):
        piece = q_ref.at[2 * origin + core, c]
        return remote(piece, piece, line_send.at[c, 0], line_recv.at[c, origin], {"tile": 2 * origin + core})

    def mate_copy(c, origin):
        slot = 2 * origin + core
        return remote(
            q_ref.at[slot, c], q_ref.at[slot, c], mate_send.at[c, origin], mate_recv.at[c, origin], {"tile": mate}
        )

    for c in range(chans):

        @pl.when(jnp.logical_not(is_root & (at == c)))
        def _():
            spread(c, 1).wait_recv()

        w = res_ref[c, :, :spectra]
        a = res_ref[c, :, 256 : 256 + spectra]
        b = res_ref[c, :, 512:640]
        parts = split3(a)
        on_re = fold3(plain(parts, parts_ref[c, 0]))
        on_im = fold3(plain(parts, parts_ref[c, 1]))
        q = jnp.concatenate([on_re[:k] - on_im[k:], on_re[k:] + on_im[:k]], axis=0)
        q_ref[me, c] = q + mix(b[:k], b[k:], start, k)
        for d in (2, 1, 3) if line == 4 else range(1, line):
            line_copy(c, d).start()
        mate_copy(c, z).start()
        turned = jnp.concatenate([-w[k:], w[:k]], axis=0)
        chosen = jnp.zeros((2 * k, rows), jnp.float32)
        for j in range(tile):
            t = (j % 2) * (tile // 2) + j // 2
            lanes = slice(j * block, (j + 1) * block)
            pair = jnp.concatenate([w[:, lanes], turned[:, lanes]], axis=1)
            chosen = jnp.where(me == t, pair, chosen)
        left_ref[c] = chosen

    for c in range(chans):
        for d in (1, 3, 2) if line == 4 else range(1, line):
            origin = lax.rem(z + d, line)
            line_arrival(c, origin).wait_recv()
            mate_copy(c, origin).start()

    for c in range(chans):
        for origin in range(line):
            mate_copy(c, origin).wait()
        for d in range(1, line):
            line_copy(c, d).wait_send()

    def drain(j, carry):
        for d in range(1, freq):
            handover(j, d).wait_send()

        b = block_at(j)

        @pl.when(b != me)
        def _():
            for d in range(freq):
                forward(j, d, b).wait_send()
                piece = own_ref.at[b, d]
                remote(piece, piece, z_send.at[j, d], z_recv.at[b, d], {"tile": b}).wait_recv()

        @pl.when(b == me)
        def _():
            for d in range(freq):
                keep(j, d).wait()

        return carry

    lax.fori_loop(0, tile, drain, 0)
    for c in range(chans):
        to_mate(c).wait_send()

        @pl.when(z != root_line(c))
        def _():
            to_root(c, 1).wait_send()

        @pl.when((z == root_line(c)) & (core != c // 2))
        def _():
            join(c).wait_send()

    @pl.when(is_root)
    def _():
        for d in range(1, tile):
            spread(at, d).wait_send()


def exact(left, right):
    return lax.dot_general(
        left, right, (((1,), (1,)), ((), ())), precision=highest, preferred_element_type=jnp.float32
    )


def build_table(ids_ref, table_ref):
    channels = ids_ref.shape[0]
    count = 2 * channels
    length = TAPS * P_SIZE
    tap = lax.broadcasted_iota(jnp.int32, (8, P_SIZE), 0)
    point = lax.broadcasted_iota(jnp.int32, (8, P_SIZE), 1)
    offsets = (tap * P_SIZE + point).astype(jnp.float32)
    shifted = math.pi * ((offsets + 0.5 - length / 2.0) / P_SIZE)
    shape = jnp.sin(shifted) / shifted
    shape = shape * (0.5 - 0.5 * jnp.cos(2.0 * math.pi * (offsets + 0.5) / length))
    shape = jnp.where(tap < TAPS, shape, 0.0)
    total = jnp.sum(jnp.sum(shape * shape, axis=1, keepdims=True), axis=0, keepdims=True)
    shape = shape / jnp.sqrt(total)
    part = lax.broadcasted_iota(jnp.int32, (count, P_SIZE), 0)
    place = lax.broadcasted_iota(jnp.int32, (count, P_SIZE), 1)
    ids = jnp.zeros((count, P_SIZE), jnp.int32)
    for c in range(channels):
        ids = jnp.where(part // 2 == c, ids_ref[c], ids)
    phases = jnp.bitwise_and(ids * place, P_SIZE - 1)
    angles = 2.0 * math.pi / P_SIZE * phases.astype(jnp.float32)
    rotors = jnp.where(jnp.bitwise_and(part, 1) == 0, jnp.cos(angles), -jnp.sin(angles))
    spread = []
    for m in range(TAPS):
        taps = rotors * shape[m : m + 1]
        spread.append(jnp.broadcast_to(taps[:, None, :], (count, SUB, P_SIZE)))
    at = lax.broadcasted_iota(jnp.int32, (count, SUB, P_SIZE), 1)
    for frame in range(SUB + TAPS - 1):
        value = jnp.zeros((count, SUB, P_SIZE), jnp.float32)
        for m in range(TAPS):
            if 0 <= frame - m < SUB:
                value = jnp.where(at == frame - m, spread[m], value)
        table_ref[:, frame * P_SIZE : (frame + 1) * P_SIZE] = value.reshape(count * SUB, P_SIZE).astype(jnp.bfloat16)


def iterate(full, gram0, k, spectra):
    fold = spectra - 128
    count = spectra // 2
    lane = lax.broadcasted_iota(jnp.int32, (1, 128), 1)

    def unfold(top, bent):
        low = jnp.where(lane < fold, bent, 0.0)
        high = jnp.where(lane < fold, pltpu.roll(bent, 128 - fold, 1), 0.0)
        return jnp.concatenate([top, jnp.concatenate([low, high], axis=0)], axis=1)

    packed = unfold(full[:spectra], full[spectra : spectra + count])
    at = spectra + count
    w = unfold(full[at : at + 2 * k], full[at + 2 * k : at + 3 * k])
    packed = jnp.concatenate([packed, jnp.zeros((256 - spectra, 256), jnp.float32)], axis=0)
    turned = packed.T
    row = lax.broadcasted_iota(jnp.int32, (256, 256), 0)
    col = lax.broadcasted_iota(jnp.int32, (256, 256), 1)
    k_re = jnp.where(row >= col, packed, turned)
    k_im = jnp.where(row < col, packed, jnp.where(row > col, -turned, 0.0))
    both = jnp.concatenate([k_re, k_im], axis=1)
    high = both.astype(jnp.bfloat16)
    rest = both - high.astype(jnp.float32)
    mid = rest.astype(jnp.bfloat16)
    low = (rest - mid.astype(jnp.float32)).astype(jnp.bfloat16)
    n2 = 2 * k
    a = jnp.zeros((n2, 256), jnp.float32)
    b = jnp.where(
        lax.broadcasted_iota(jnp.int32, (n2, 128), 0) == lax.broadcasted_iota(jnp.int32, (n2, 128), 1), 1.0, 0.0
    )
    b = jnp.where(lax.broadcasted_iota(jnp.int32, (n2, 128), 0) < k, b, 0.0)
    held = gram0
    for _ in range(ITERS):
        w3 = split3(w)
        on_high = plain(w3, high)
        on_mid = plain(w3[: 2 * n2], mid)
        on_low = plain(w3[:n2], low)
        kw = (on_low + on_mid[n2:] + on_high[2 * n2 :]) + (on_mid[:n2] + on_high[n2 : 2 * n2]) + on_high[:n2]
        on_re, on_im = kw[:, :256], kw[:, 256:]
        kw = jnp.concatenate([on_re[:k] + on_im[k:], on_re[k:] - on_im[:k]], axis=0)
        y = kw / spectra + loading * w
        u = (y + loading * w) / spectra
        g_re = exact(w, u[:k])
        g_im = exact(w, u[k:])
        gram = jnp.concatenate([g_re[:k] + g_im[k:], g_im[:k] - g_re[k:]], axis=0) + loading * loading * held
        m_re, m_im = inverse_factor(gram, k)
        grown = jnp.concatenate([y, w / spectra + loading * a, loading * b], axis=1)
        grown = mix(m_re, m_im, grown, k)
        w, a, b = grown[:, :256], grown[:, 256:512], grown[:, 512:]
        held = b_identity(n2, k)
    return jnp.concatenate([w, a, b], axis=1)


def b_identity(n2, k):
    row = lax.broadcasted_iota(jnp.int32, (n2, k), 0)
    col = lax.broadcasted_iota(jnp.int32, (n2, k), 1)
    return jnp.where(row == col, 1.0, 0.0)


def finish_kernel(own_ref, q_ref, left_ref, out_ref):
    tile, _, chans, rows, cols = own_ref.shape
    block = rows // 2
    n2 = q_ref.shape[2]
    for c in range(chans):
        w3 = split3(left_ref[c])
        w_left = jnp.concatenate([w3[:n2], w3[:n2], w3[n2 : 2 * n2], w3[n2 : 2 * n2], w3[:n2], w3[2 * n2 :]], axis=0)
        for t in range(tile):
            s3 = split3(q_ref[t, c])
            s_right = jnp.concatenate(
                [s3[:n2], s3[n2 : 2 * n2], s3[:n2], s3[n2 : 2 * n2], s3[2 * n2 :], s3[:n2]], axis=0
            )
            cleaned = own_ref[t, 0, c].astype(jnp.float32) - tn(w_left, s_right)
            out_ref[0, c, :, t * cols : (t + 1) * cols] = cleaned[:block]
            out_ref[1, c, :, t * cols : (t + 1) * cols] = cleaned[block:]


def channelize_kernel(volts_ref, table_ref, out_ref):
    step = pl.program_id(0)
    span = (STEP + TAPS - 1) * P_SIZE
    start = pl.multiple_of(step * (STEP * P_SIZE), P_SIZE)
    chunk = volts_ref[:, pl.ds(start, span)]
    result = nt(table_ref[...], chunk)
    out_ref[...] = result.reshape(out_ref.shape).astype(jnp.bfloat16)


def channelize(voltages, table, rows, spectra_all):
    inputs_local, samples = voltages.shape
    return pl.pallas_call(
        channelize_kernel,
        grid=(spectra_all // STEP,),
        in_specs=[VMEM, VMEM],
        out_specs=pl.BlockSpec((rows, STEP, inputs_local), lambda i: (0, i, 0)),
        out_shape=jax.ShapeDtypeStruct((rows, spectra_all, inputs_local), jnp.bfloat16),
        compiler_params=pltpu.CompilerParams(vmem_limit_bytes=40 * 2**20),
    )(voltages, table)


def start_kernel(v_ref, q_ref, pg_ref, *, k, lanes):
    chans, _, spectra, _ = v_ref.shape
    pg_ref[...] = jnp.zeros_like(pg_ref)
    for c in range(chans):
        pg_ref[2 * k * c : 2 * k * (c + 1), :spectra] = project(q_ref[...], v_ref[c, 0], v_ref[c, 1], k)


def step_kernel(v_ref, z_ref, pg_ref, z_out, pg_out, *, k, lanes, first):
    chans, _, spectra, width = v_ref.shape
    pg_out[...] = jnp.zeros_like(pg_out)
    for c in range(chans):
        at = slice(2 * k * c, 2 * k * (c + 1))
        weights = pg_ref[at, :spectra]
        basis = z_ref[...] if first else z_ref[c]
        if not first:
            m_re, m_im = inverse_factor(pg_ref[at, lanes:], k)
            weights = mix(m_re, m_im, weights, k)
            basis = mix(m_re, m_im, basis, k)
        real_v, imag_v = v_ref[c, 0], v_ref[c, 1]
        parts = split3(weights / spectra)
        on_re = fold3(plain(parts, real_v))
        on_im = fold3(plain(parts, imag_v))
        z = jnp.concatenate([on_re[:k] - on_im[k:], on_re[k:] + on_im[:k]], axis=0) + loading * basis
        z_out[c] = z
        pg_out[at, :spectra] = project(z, real_v, imag_v, k)
        pad = jnp.zeros((lanes_pad(k), width), jnp.float32)
        right = jnp.concatenate([z[:k], pad], axis=0)
        right_im = jnp.concatenate([z[k:], pad], axis=0)
        dims = (((1,), (1,)), ((), ()))
        first_dot = lax.dot_general(z, right, dims, precision=highest, preferred_element_type=jnp.float32)
        second_dot = lax.dot_general(z, right_im, dims, precision=highest, preferred_element_type=jnp.float32)
        g_re = first_dot[:k] + second_dot[k:]
        g_im = second_dot[:k] - first_dot[k:]
        pg_out[at, lanes:] = jnp.concatenate([g_re, g_im], axis=0)


def lanes_pad(k):
    return 128 - k


def clean_kernel(v_ref, z_ref, pg_ref, out_ref, *, k, lanes):
    chans, _, spectra, width = v_ref.shape
    parts_count, _, _, block, _ = out_ref.shape
    for c in range(chans):
        at = slice(2 * k * c, 2 * k * (c + 1))
        m_re, m_im = inverse_factor(pg_ref[at, lanes:], k)
        w = mix(m_re, m_im, pg_ref[at, :spectra], k)
        q = mix(m_re, m_im, z_ref[c], k)
        turned = jnp.concatenate([q[k:], -q[:k]], axis=0)
        w3 = split3(w)
        n2 = 2 * k
        w_left = jnp.concatenate([w3[:n2], w3[:n2], w3[n2 : 2 * n2], w3[n2 : 2 * n2], w3[:n2], w3[2 * n2 :]], axis=0)
        for r, side in ((0, q), (1, turned)):
            s3 = split3(side)
            s_right = jnp.concatenate(
                [s3[:n2], s3[n2 : 2 * n2], s3[:n2], s3[n2 : 2 * n2], s3[2 * n2 :], s3[:n2]], axis=0
            )
            fitted = tn(w_left, s_right)
            cleaned = v_ref[c, r].astype(jnp.float32) - fitted
            out_ref[:, r, c] = cleaned.reshape(parts_count, block, width).astype(jnp.bfloat16)


def reduce_kernel(x_ref, out_ref, land_ref, send1, recv1, send2, recv2, *, size, chunk):
    me = lax.axis_index("tile")
    barrier = pltpu.get_barrier_semaphore()
    for d in range(1, size):
        peer = lax.rem(me + d, size)
        pl.semaphore_signal(barrier, inc=1, device_id={"tile": peer}, device_id_type=MESH)
    pl.semaphore_wait(barrier, size - 1)
    mine = pl.ds(pl.multiple_of(me * chunk, 8), chunk)
    sends = []
    for d in range(1, size):
        peer = lax.rem(me + d, size)
        copy = pltpu.make_async_remote_copy(
            src_ref=x_ref.at[pl.ds(pl.multiple_of(peer * chunk, 8), chunk)],
            dst_ref=land_ref.at[d - 1],
            send_sem=send1.at[d - 1],
            recv_sem=recv1.at[d - 1],
            device_id={"tile": peer},
            device_id_type=MESH,
        )
        copy.start()
        sends.append(copy)
    total = x_ref[mine]
    for d in range(1, size):
        sends[d - 1].wait_recv()
        total = total + land_ref[d - 1]
    out_ref[mine] = total
    later = []
    for d in range(1, size):
        peer = lax.rem(me + d, size)
        copy = pltpu.make_async_remote_copy(
            src_ref=out_ref.at[mine],
            dst_ref=out_ref.at[mine],
            send_sem=send2.at[d - 1],
            recv_sem=recv2.at[d - 1],
            device_id={"tile": peer},
            device_id_type=MESH,
        )
        copy.start()
        later.append(copy)
    for copy in later:
        copy.wait_recv()
    for copy in sends + later:
        copy.wait_send()


def tile_sum(x, size):
    rows, width = x.shape
    chunk = rows // size
    return pl.pallas_call(
        functools.partial(reduce_kernel, size=size, chunk=chunk),
        in_specs=[VMEM],
        out_specs=VMEM,
        out_shape=jax.ShapeDtypeStruct(x.shape, jnp.float32),
        scratch_shapes=[pltpu.VMEM((size - 1, chunk, width), jnp.float32)]
        + [pltpu.SemaphoreType.DMA((size - 1,))] * 4,
        compiler_params=pltpu.CompilerParams(collective_id=0, has_side_effects=True),
    )(x)


def up(value, unit):
    return -(-value // unit) * unit


def body_split(voltages, channel_ids, start_basis):
    inputs_local, samples_count = voltages.shape
    freq_count = lax.axis_size("freq")
    tile_count = lax.axis_size("tile")
    channels = channel_ids.shape[0]
    chan_local = channels // freq_count
    spectra_all = samples_count // P_SIZE - TAPS + 1
    spectra_local = spectra_all // tile_count
    k = start_basis.shape[1]
    width = freq_count * inputs_local

    coeffs = make_table(channel_ids, TAPS, P_SIZE).reshape(TAPS, 2 * channels, P_SIZE)
    local = channelize(voltages, banded(coeffs), 2 * channels, spectra_all)
    parcel = local.reshape(2, freq_count, chan_local, spectra_all, inputs_local)
    arrived = lax.all_to_all(parcel, "freq", split_axis=1, concat_axis=1, tiled=True)
    values = jnp.transpose(arrived, (2, 0, 3, 1, 4)).reshape(chan_local, 2, spectra_all, width)

    mine = lax.axis_index("tile")
    start = start_basis.reshape(2 * k, freq_count, tile_count, inputs_local)
    start = lax.dynamic_index_in_dim(start, mine, 2, keepdims=False).reshape(2 * k, width)

    lanes = up(spectra_all, 128)
    chunk = up(-(-chan_local * 2 * k // tile_count), 8)
    packed = jax.ShapeDtypeStruct((tile_count * chunk, lanes + 128), jnp.float32)
    z_shape = jax.ShapeDtypeStruct((chan_local, 2 * k, width), jnp.float32)
    params = pltpu.CompilerParams(vmem_limit_bytes=40 * 2**20)

    partial = pl.pallas_call(
        functools.partial(start_kernel, k=k, lanes=lanes),
        in_specs=[VMEM] * 2, out_specs=VMEM, out_shape=packed, compiler_params=params,
    )(values, start)
    z = start
    for step_at in range(ITERS):
        total = tile_sum(partial, tile_count)
        z, partial = pl.pallas_call(
            functools.partial(step_kernel, k=k, lanes=lanes, first=step_at == 0),
            in_specs=[VMEM] * 3, out_specs=[VMEM] * 2, out_shape=[z_shape, packed],
            compiler_params=params,
        )(values, z, total)
    total = tile_sum(partial, tile_count)
    cleaned = pl.pallas_call(
        functools.partial(clean_kernel, k=k, lanes=lanes),
        in_specs=[VMEM] * 3, out_specs=VMEM,
        out_shape=jax.ShapeDtypeStruct((tile_count, 2, chan_local, spectra_local, width), jnp.bfloat16),
        compiler_params=params,
    )(values, z, total)
    moved = lax.all_to_all(cleaned, "tile", split_axis=0, concat_axis=0, tiled=True)
    moved = moved.reshape(tile_count, 2, chan_local, spectra_local, freq_count, inputs_local)
    moved = jnp.transpose(moved, (1, 2, 3, 4, 0, 5)).astype(jnp.float32)
    return moved.reshape(2, chan_local, spectra_local, freq_count * tile_count * inputs_local)


def body(voltages, channel_ids, start_basis):
    inputs_local, samples_count = voltages.shape
    freq_count = lax.axis_size("freq")
    tile_count = lax.axis_size("tile")
    if inputs_local % 128:
        return body_split(voltages, channel_ids, start_basis)
    channels = channel_ids.shape[0]
    chan_local = channels // freq_count
    spectra_all = samples_count // P_SIZE - TAPS + 1
    spectra_local = spectra_all // tile_count
    k = start_basis.shape[1]
    width = freq_count * inputs_local
    if spectra_all != 192 or spectra_local % SUB or tile_count % 4 or chan_local > 4 or k != 8:
        return body_split(voltages, channel_ids, start_basis)

    start = start_basis.reshape(2 * k, freq_count * tile_count * inputs_local)
    rows = 2 * spectra_local
    line = tile_count // 2
    half = up(spectra_all + spectra_all // 2 + 3 * k, 16) // 2
    sem = pltpu.SemaphoreType.DMA
    peers = freq_count - 1
    own, q, left = pl.pallas_call(
        functools.partial(fused_kernel, k=k, freq=freq_count, tile=tile_count),
        in_specs=[pl.BlockSpec(memory_space=pl.ANY), pl.BlockSpec(memory_space=pltpu.SMEM), VMEM],
        out_specs=[pl.BlockSpec(memory_space=pl.ANY), VMEM, VMEM],
        out_shape=[
            jax.ShapeDtypeStruct((tile_count, freq_count, chan_local, rows, inputs_local), jnp.bfloat16),
            jax.ShapeDtypeStruct((tile_count, chan_local, 2 * k, width), jnp.float32),
            jax.ShapeDtypeStruct((chan_local, 2 * k, rows), jnp.float32),
        ],
        scratch_shapes=[
            pltpu.VMEM((tile_count, inputs_local, (spectra_local + TAPS - 1) * P_SIZE), jnp.bfloat16),
            pltpu.VMEM((2 * channels * SUB, (SUB + TAPS - 1) * P_SIZE), jnp.bfloat16),
            pltpu.VMEM((tile_count, freq_count, chan_local, rows, inputs_local), jnp.bfloat16),
            pltpu.VMEM((tile_count, freq_count, chan_local, rows, inputs_local), jnp.bfloat16),
            pltpu.VMEM((chan_local, 2, spectra_all, width), jnp.bfloat16),
            pltpu.VMEM((chan_local, 2, half, 128), jnp.float32),
            pltpu.VMEM((chan_local, half, 128), jnp.float32),
            pltpu.VMEM((chan_local, half, 128), jnp.float32),
            pltpu.VMEM((chan_local, line - 1, half, 128), jnp.float32),
            pltpu.VMEM((2, half, 128), jnp.float32),
            pltpu.VMEM((chan_local, 2 * k, 640), jnp.float32),
            sem((tile_count,)), sem((tile_count,)), sem((freq_count,)),
            sem((tile_count, peers)), sem((tile_count, peers)),
            sem((tile_count, freq_count)), sem((tile_count, freq_count)),
            sem((chan_local,)), sem((chan_local,)),
            sem((chan_local,)), sem((chan_local, line - 1)),
            sem((chan_local,)), sem((chan_local,)),
            sem((tile_count - 1,)), sem((chan_local,)),
            sem((chan_local, line - 1)), sem((chan_local, line)),
            sem((chan_local, line)), sem((chan_local, line)),
        ],
        compiler_params=pltpu.CompilerParams(
            collective_id=0, has_side_effects=True, vmem_limit_bytes=56 * 2**20
        ),
    )(voltages, channel_ids, start)
    stride = tile_count * inputs_local
    return pl.pallas_call(
        finish_kernel,
        grid=(freq_count,),
        in_specs=[
            pl.BlockSpec((tile_count, 1, chan_local, rows, inputs_local), lambda f: (0, f, 0, 0, 0)),
            pl.BlockSpec((tile_count, chan_local, 2 * k, inputs_local), lambda f: (0, 0, 0, f)),
            pl.BlockSpec((chan_local, 2 * k, rows), lambda f: (0, 0, 0)),
        ],
        out_specs=pl.BlockSpec((2, chan_local, spectra_local, stride), lambda f: (0, 0, 0, f)),
        out_shape=jax.ShapeDtypeStruct((2, chan_local, spectra_local, freq_count * stride), jnp.float32),
        compiler_params=pltpu.CompilerParams(vmem_limit_bytes=60 * 2**20),
    )(own, q, left)


def solution(mesh):
    in_specs = (P(("freq", "tile"), None), P(), P())
    out_specs = P(None, "freq", "tile", None)
    return jax.shard_map(body, mesh=mesh, in_specs=in_specs, out_specs=out_specs, check_vma=False)
```

```python
import functools
import math

import jax
import jax.numpy as jnp
from jax import lax
from jax.experimental import pallas as pl
from jax.experimental.pallas import tpu as pltpu
from jax.sharding import PartitionSpec as P

TAPS = 4
P_SIZE = 128
ITERS = 3
STEP = 16
SUB = 8
EARLY = 4
AHEAD = 5
LATE = 6

loading = 0.5
highest = lax.Precision.HIGHEST
VMEM = pl.BlockSpec(memory_space=pltpu.VMEM)
MESH = pl.DeviceIdType.MESH


def make_table(channel_ids, taps_count, points):
    length = taps_count * points
    offsets = jnp.arange(length, dtype=jnp.float32)
    shifted = (offsets + 0.5 - length / 2.0) / points
    window = jnp.sinc(shifted) * (0.5 - 0.5 * jnp.cos(2.0 * math.pi * (offsets + 0.5) / length))
    window = window / jnp.sqrt(jnp.sum(window * window))
    window = window.reshape(taps_count, points)
    phases = channel_ids[:, None] * jnp.arange(points, dtype=jnp.int32)[None, :] % points
    angles = 2.0 * math.pi / points * phases.astype(jnp.float32)
    rotors = jnp.stack([jnp.cos(angles), -jnp.sin(angles)])
    return (window[:, None, None, :] * rotors[None]).astype(jnp.bfloat16)


def banded(coeffs):
    rows = coeffs.shape[1]
    spect = lax.broadcasted_iota(jnp.int32, (1, STEP, STEP + TAPS - 1, 1), 1)
    frame = lax.broadcasted_iota(jnp.int32, (1, STEP, STEP + TAPS - 1, 1), 2)
    table = jnp.zeros((rows, STEP, STEP + TAPS - 1, P_SIZE), jnp.bfloat16)
    for tap in range(TAPS):
        table = jnp.where(frame - spect == tap, coeffs[tap][:, None, None, :], table)
    return table.reshape(rows * STEP, (STEP + TAPS - 1) * P_SIZE)


def nt(left, right):
    return lax.dot_general(left, right, (((1,), (1,)), ((), ())), preferred_element_type=jnp.float32)


def split3(value):
    high = value.astype(jnp.bfloat16)
    rest = value - high.astype(jnp.float32)
    mid = rest.astype(jnp.bfloat16)
    low = (rest - mid.astype(jnp.float32)).astype(jnp.bfloat16)
    return jnp.concatenate([high, mid, low], axis=0)


def fold3(value):
    rows = value.shape[0] // 3
    return value[:rows] + value[rows : 2 * rows] + value[2 * rows :]


def plain(left, right):
    return lax.dot_general(left, right, (((1,), (0,)), ((), ())), preferred_element_type=jnp.float32)


def project(z, real_v, imag_v, k):
    parts = split3(z)
    on_re = fold3(nt(parts, real_v))
    on_im = fold3(nt(parts, imag_v))
    return jnp.concatenate([on_re[:k] + on_im[k:], on_re[k:] - on_im[:k]], axis=0)


def inverse_factor(gram, k, off=0):
    lanes = gram.shape[1]
    col = lax.broadcasted_iota(jnp.int32, (k, lanes), 1)
    row = lax.broadcasted_iota(jnp.int32, (k, lanes), 0)
    zero = jnp.zeros((k, lanes), jnp.float32)
    a_re = gram[:k]
    a_im = gram[k:]
    m_re = jnp.where(col == row, 1.0, zero)
    m_im = zero
    for j in range(k):
        at_col = col == j + off
        c_re = jnp.sum(jnp.where(at_col, a_re, 0.0), axis=1, keepdims=True)
        c_im = jnp.sum(jnp.where(at_col, a_im, 0.0), axis=1, keepdims=True)
        pivot = jnp.sqrt(c_re[j : j + 1])
        l_re = jnp.where(row[:, :1] > j, c_re / pivot, 0.0)
        l_im = jnp.where(row[:, :1] > j, c_im / pivot, 0.0)
        ar, ai = a_re[j : j + 1] / pivot, a_im[j : j + 1] / pivot
        mr, mi = m_re[j : j + 1] / pivot, m_im[j : j + 1] / pivot
        here = row == j
        a_re = jnp.where(here, ar, a_re - (l_re * ar - l_im * ai))
        a_im = jnp.where(here, ai, a_im - (l_re * ai + l_im * ar))
        m_re = jnp.where(here, mr, m_re - (l_re * mr - l_im * mi))
        m_im = jnp.where(here, mi, m_im - (l_re * mi + l_im * mr))
    return m_re, -m_im


def mix(m_re, m_im, rows, k):
    out_re = jnp.zeros((k, rows.shape[1]), jnp.float32)
    out_im = jnp.zeros((k, rows.shape[1]), jnp.float32)
    for j in range(k):
        f_re, f_im = m_re[:, j : j + 1], m_im[:, j : j + 1]
        r_re, r_im = rows[j : j + 1], rows[k + j : k + j + 1]
        out_re = out_re + (f_re * r_re - f_im * r_im)
        out_im = out_im + (f_re * r_im + f_im * r_re)
    return jnp.concatenate([out_re, out_im], axis=0)


def tn(left, right):
    return lax.dot_general(left, right, (((0,), (0,)), ((), ())), preferred_element_type=jnp.float32)


def fused_kernel(
    volts_hbm, ids_ref, start_ref, own_ref, q_ref, left_ref,
    vol_ref, table_ref, stage, v_ref, parts_ref, pack_ref, pair_ref, half_ref, land_ref, full_ref, res_ref,
    vol_sem, own_sem, mine_sem, f_send, f_recv, z_send, z_recv,
    p_send, p_recv, k_send, k_recv, j_send, j_recv, b_send, b_recv,
    line_send, line_recv, mate_send, mate_recv,
    *, k, freq, tile,
):
    chans, _, spectra, width = parts_ref.shape
    cols = vol_ref.shape[1]
    block = spectra // tile
    rows = 2 * block
    subs = block // SUB
    window = vol_ref.shape[2]
    group = lax.axis_index("freq")
    me = lax.axis_index("tile")
    line = tile // 2
    z, core = me // 2, lax.rem(me, 2)
    mate = me + 1 - 2 * core
    barrier = pltpu.get_barrier_semaphore()
    for d in range(1, freq):
        pl.semaphore_signal(barrier, inc=1, device_id={"freq": lax.rem(group + d, freq)}, device_id_type=MESH)
    for d in range(1, tile):
        pl.semaphore_signal(barrier, inc=1, device_id={"tile": lax.rem(me + d, tile)}, device_id_type=MESH)

    def remote(src, dst, send, recv, where):
        return pltpu.make_async_remote_copy(
            src_ref=src, dst_ref=dst, send_sem=send, recv_sem=recv, device_id=where, device_id_type=MESH
        )

    def block_at(j):
        return lax.rem(j, 2) * (tile // 2) + j // 2

    def fetch(j):
        lanes = pl.ds(pl.multiple_of(block_at(j) * (block * P_SIZE), P_SIZE), window)
        return pltpu.make_async_copy(volts_hbm.at[:, lanes], vol_ref.at[j], vol_sem.at[j])

    for j in range(tile):
        fetch(j).start()

    build_table(ids_ref, table_ref)

    def handover(j, d):
        peer = lax.rem(group + d, freq)
        return remote(
            stage.at[j, peer], v_ref.at[j, group],
            f_send.at[j, d - 1], f_recv.at[j, d - 1], {"freq": peer},
        )

    def own_part(j):
        return pltpu.make_async_copy(stage.at[j, group], v_ref.at[j, group], own_sem.at[j])

    def filter_step(j):
        fetch(j).wait()
        span = (SUB + TAPS - 1) * P_SIZE
        right = jnp.concatenate(
            [vol_ref[j, :, n * SUB * P_SIZE : n * SUB * P_SIZE + span] for n in range(subs)], axis=0
        )
        result = nt(table_ref[...], right)
        pieces = [result[:, n * cols : (n + 1) * cols].reshape(-1, SUB, cols) for n in range(subs)]
        result = jnp.concatenate(pieces, axis=1)
        stage[j] = result.reshape(freq, chans, rows, cols).astype(jnp.bfloat16)

    def arrive(j):
        for d in range(1, freq):
            handover(j, d).wait_recv()
        own_part(j).wait()

    def forward(j, d, b):
        f = lax.rem(group + d, freq)
        src = stage.at[j, group] if d == 0 else v_ref.at[j, f]
        return remote(src, own_ref.at[me, f], z_send.at[j, d], z_recv.at[me, f], {"tile": b})

    def keep(j, d):
        f = lax.rem(group + d, freq)
        src = stage.at[j, group] if d == 0 else v_ref.at[j, f]
        return pltpu.make_async_copy(src, own_ref.at[me, f], mine_sem.at[d])

    def pass_on(j, d):
        b = block_at(j)

        @pl.when(b != me)
        def _():
            forward(j, d, b).start()

        @pl.when(b == me)
        def _():
            keep(j, d).start()

    def compute(j, carry):
        filter_step(j)
        return carry

    def dispatch(j, carry):
        for d in range(1, freq):
            handover(j, d).start()
        own_part(j).start()
        pass_on(j, 0)
        return carry

    def collect(j, carry):
        arrive(j)

        @pl.when(j < EARLY)
        def _():
            for d in range(1, freq):
                pass_on(j, d)

        return carry

    def pace(j, carry):
        filter_step(j)
        return dispatch(j, carry)

    lax.fori_loop(0, AHEAD, compute, 0)
    pl.semaphore_wait(barrier, freq - 1 + tile - 1)
    lax.fori_loop(0, AHEAD, dispatch, 0)
    lax.fori_loop(AHEAD, tile, pace, 0)

    start = jnp.concatenate(
        [
            start_ref[:, pl.ds(pl.multiple_of(f * (tile * cols) + me * cols, cols), cols)]
            for f in range(freq)
        ],
        axis=1,
    )
    start3 = split3(start)
    stages, heights, offsets, first = plan(spectra, block, k)

    def at_stage(g):
        return pl.ds(offsets[g], heights[g])

    def to_mate(g, c):
        return remote(
            pack_ref.at[c, 1 - core, at_stage(g)], pair_ref.at[c, at_stage(g)],
            p_send.at[g, c], p_recv.at[g, c], {"tile": mate},
        )

    def root_line(c):
        return line // 2 - 1 + c % 2

    def to_root(g, c, d):
        return remote(
            half_ref.at[c, at_stage(g)], land_ref.at[c, d - 1, at_stage(g)],
            k_send.at[g, c], k_recv.at[g, c, d - 1], {"tile": 2 * root_line(c) + core},
        )

    def product(g, c):
        low, high = stages[g]
        n = (high - low) * block
        loose = [
            v_ref[:high, f, c].astype(jnp.float32).reshape(high, 2, block, cols) for f in range(freq)
        ]
        real_f, imag_f = [
            jnp.concatenate([part[:, r].reshape(high * block, cols) for part in loose], axis=1) for r in range(2)
        ]
        if high == tile:
            parts_ref[c, 0] = real_f.astype(jnp.bfloat16)
            parts_ref[c, 1] = imag_f.astype(jnp.bfloat16)
        real_n, imag_n = real_f[low * block :], imag_f[low * block :]
        blank = jnp.zeros((128 - n, width), jnp.float32)
        real_w = jnp.concatenate([real_n, blank], axis=0).astype(jnp.bfloat16)
        imag_w = jnp.concatenate([imag_n, blank], axis=0).astype(jnp.bfloat16)
        left_re, left_im = real_n.astype(jnp.bfloat16), imag_n.astype(jnp.bfloat16)
        if low == 0:
            k_re = nt(left_re, real_w) + nt(left_im, imag_w)
            k_im = nt(left_re, imag_w) - nt(left_im, real_w)
            row = lax.broadcasted_iota(jnp.int32, (n, 128), 0)
            col = lax.broadcasted_iota(jnp.int32, (n, 128), 1)
            body = [jnp.where(row >= col, k_re, k_im)]
        else:
            gap = [jnp.zeros((spectra - high * block, width), jnp.float32)] if high < tile else []
            on_re = jnp.concatenate([real_f] + gap + [imag_f] + gap, axis=0).astype(jnp.bfloat16)
            on_im = jnp.concatenate([imag_f] + gap + [-real_f] + gap, axis=0).astype(jnp.bfloat16)
            wide = nt(left_re, on_re) + nt(left_im, on_im)
            body = [wide[:, m : m + 128] for m in range(0, 2 * spectra, 128)]
        on_re = fold3(nt(start3, real_w))
        on_im = fold3(nt(start3, imag_w))
        body += [on_re[:k] + on_im[k:], on_re[k:] - on_im[:k]]
        tail = 2 * heights[g] - sum(piece.shape[0] for piece in body)
        if tail:
            body.append(jnp.zeros((tail, 128), jnp.float32))
        pack_ref[c, :, at_stage(g)] = jnp.concatenate(body, axis=0).reshape(2, heights[g], 128)
        to_mate(g, c).start()

    for g, (low, high) in enumerate(stages):
        lax.fori_loop(low, high, collect, 0)
        for c in range(chans):
            product(g, c)
        for c in range(chans):
            to_mate(g, c).wait_recv()
            half_ref[c, at_stage(g)] = pack_ref[c, core, at_stage(g)] + pair_ref[c, at_stage(g)]
            for d in range(1, line):

                @pl.when(z == (root_line(c) + d) % line)
                def _():
                    to_root(g, c, d).start()

    side = z - (line // 2 - 1)
    at = side + 2 * core
    is_root = (side >= 0) & (side < 2) & (at < chans)

    def pass_rest(j, carry):
        for d in range(1, freq):
            pass_on(j, d)
        return carry

    lax.fori_loop(EARLY, LATE, pass_rest, 0)

    @pl.when(jnp.logical_not(is_root))
    def _():
        lax.fori_loop(LATE, tile, pass_rest, 0)

    g_re = exact(start_ref[...], start_ref[:k])
    g_im = exact(start_ref[...], start_ref[k:])
    gram0 = jnp.concatenate([g_re[:k] + g_im[k:], g_im[:k] - g_re[k:]], axis=0)

    def join(g, c):
        return remote(
            half_ref.at[c, at_stage(g)], full_ref.at[core, at_stage(g)], j_send.at[g, c], j_recv.at[g, c], {"tile": mate}
        )

    for g in range(len(stages)):
        for c in range(chans):

            @pl.when(z == root_line(c))
            def _():
                total = half_ref[c, at_stage(g)]
                for d in range(1, line):
                    to_root(g, c, d).wait_recv()
                    total = total + land_ref[c, d - 1, at_stage(g)]

                @pl.when(core == c // 2)
                def _():
                    full_ref[core, at_stage(g)] = total

                @pl.when(core != c // 2)
                def _():
                    half_ref[c, at_stage(g)] = total
                    join(g, c).start()

    def spread(c, d):
        return remote(
            res_ref.at[c], res_ref.at[c], b_send.at[d - 1], b_recv.at[c], {"tile": lax.rem(me + d, tile)}
        )

    @pl.when(is_root)
    def _():
        for c in range(chans):

            @pl.when(at == c)
            def _():
                for g in range(len(stages)):
                    join(g, c).wait_recv()

        pieces = [
            full_ref[:, at_stage(g)].reshape(2 * heights[g], 128) for g in range(len(stages))
        ]
        res_ref[at] = iterate(pieces, stages, gram0, k, spectra, block)
        for d in range(1, tile):
            spread(at, d).start()
        lax.fori_loop(LATE, tile, pass_rest, 0)

    def line_copy(c, d):
        return remote(
            q_ref.at[me, c], q_ref.at[me, c], line_send.at[c, d - 1], line_recv.at[c, z],
            {"tile": lax.rem(me + 2 * d, tile)},
        )

    def line_arrival(c, origin):
        piece = q_ref.at[2 * origin + core, c]
        return remote(piece, piece, line_send.at[c, 0], line_recv.at[c, origin], {"tile": 2 * origin + core})

    def mate_copy(c, origin):
        slot = 2 * origin + core
        return remote(
            q_ref.at[slot, c], q_ref.at[slot, c], mate_send.at[c, origin], mate_recv.at[c, origin], {"tile": mate}
        )

    for c in range(chans):

        @pl.when(jnp.logical_not(is_root & (at == c)))
        def _():
            spread(c, 1).wait_recv()

        w = res_ref[c, :, :spectra]
        a = res_ref[c, :, 256 : 256 + spectra]
        b = res_ref[c, :, 512:640]
        parts = split3(a)
        on_re = fold3(plain(parts, parts_ref[c, 0]))
        on_im = fold3(plain(parts, parts_ref[c, 1]))
        q = jnp.concatenate([on_re[:k] - on_im[k:], on_re[k:] + on_im[:k]], axis=0)
        q_ref[me, c] = q + mix(b[:k], b[k:], start, k)
        for d in (2, 1, 3) if line == 4 else range(1, line):
            line_copy(c, d).start()
        mate_copy(c, z).start()
        turned = jnp.concatenate([-w[k:], w[:k]], axis=0)
        chosen = jnp.zeros((2 * k, rows), jnp.float32)
        for j in range(tile):
            t = (j % 2) * (tile // 2) + j // 2
            lanes = slice(j * block, (j + 1) * block)
            pair = jnp.concatenate([w[:, lanes], turned[:, lanes]], axis=1)
            chosen = jnp.where(me == t, pair, chosen)
        left_ref[c] = chosen

    for c in range(chans):
        for d in (1, 3, 2) if line == 4 else range(1, line):
            origin = lax.rem(z + d, line)
            line_arrival(c, origin).wait_recv()
            mate_copy(c, origin).start()

    for c in range(chans):
        for origin in range(line):
            mate_copy(c, origin).wait()
        for d in range(1, line):
            line_copy(c, d).wait_send()

    def drain(j, carry):
        for d in range(1, freq):
            handover(j, d).wait_send()

        b = block_at(j)

        @pl.when(b != me)
        def _():
            for d in range(freq):
                forward(j, d, b).wait_send()
                piece = own_ref.at[b, d]
                remote(piece, piece, z_send.at[j, d], z_recv.at[b, d], {"tile": b}).wait_recv()

        @pl.when(b == me)
        def _():
            for d in range(freq):
                keep(j, d).wait()

        return carry

    lax.fori_loop(0, tile, drain, 0)
    for g in range(len(stages)):
        for c in range(chans):
            to_mate(g, c).wait_send()

            @pl.when(z != root_line(c))
            def _():
                to_root(g, c, 1).wait_send()

            @pl.when((z == root_line(c)) & (core != c // 2))
            def _():
                join(g, c).wait_send()

    @pl.when(is_root)
    def _():
        for d in range(1, tile):
            spread(at, d).wait_send()


def exact(left, right):
    return lax.dot_general(
        left, right, (((1,), (1,)), ((), ())), precision=highest, preferred_element_type=jnp.float32
    )


def build_table(ids_ref, table_ref):
    channels = ids_ref.shape[0]
    count = 2 * channels
    length = TAPS * P_SIZE
    tap = lax.broadcasted_iota(jnp.int32, (8, P_SIZE), 0)
    point = lax.broadcasted_iota(jnp.int32, (8, P_SIZE), 1)
    offsets = (tap * P_SIZE + point).astype(jnp.float32)
    shifted = math.pi * ((offsets + 0.5 - length / 2.0) / P_SIZE)
    shape = jnp.sin(shifted) / shifted
    shape = shape * (0.5 - 0.5 * jnp.cos(2.0 * math.pi * (offsets + 0.5) / length))
    shape = jnp.where(tap < TAPS, shape, 0.0)
    total = jnp.sum(jnp.sum(shape * shape, axis=1, keepdims=True), axis=0, keepdims=True)
    shape = shape / jnp.sqrt(total)
    part = lax.broadcasted_iota(jnp.int32, (count, P_SIZE), 0)
    place = lax.broadcasted_iota(jnp.int32, (count, P_SIZE), 1)
    ids = jnp.zeros((count, P_SIZE), jnp.int32)
    for c in range(channels):
        ids = jnp.where(part // 2 == c, ids_ref[c], ids)
    phases = jnp.bitwise_and(ids * place, P_SIZE - 1)
    angles = 2.0 * math.pi / P_SIZE * phases.astype(jnp.float32)
    rotors = jnp.where(jnp.bitwise_and(part, 1) == 0, jnp.cos(angles), -jnp.sin(angles))
    spread = []
    for m in range(TAPS):
        taps = rotors * shape[m : m + 1]
        spread.append(jnp.broadcast_to(taps[:, None, :], (count, SUB, P_SIZE)))
    at = lax.broadcasted_iota(jnp.int32, (count, SUB, P_SIZE), 1)
    for frame in range(SUB + TAPS - 1):
        value = jnp.zeros((count, SUB, P_SIZE), jnp.float32)
        for m in range(TAPS):
            if 0 <= frame - m < SUB:
                value = jnp.where(at == frame - m, spread[m], value)
        table_ref[:, frame * P_SIZE : (frame + 1) * P_SIZE] = value.reshape(count * SUB, P_SIZE).astype(jnp.bfloat16)


def plan(spectra, block, k):
    blocks = spectra // block
    first = 128 // block
    stages = [(0, first)] + [(j, j + 1) for j in range(first, blocks)]
    heights = [up(first * block + 2 * k, 16) // 2]
    heights += [up(2 * spectra // 128 * block + 2 * k, 16) // 2] * (blocks - first)
    offsets = [sum(heights[:g]) for g in range(len(heights))]
    return stages, heights, offsets, first * block


def iterate(pieces, stages, gram0, k, spectra, block):
    first = stages[0][1] * block
    tiles = 2 * spectra // 128
    wide = jnp.concatenate(
        [
            jnp.concatenate([piece[m * block : (m + 1) * block] for m in range(tiles)], axis=1)
            for piece in pieces[1:]
        ],
        axis=0,
    )
    pad = 256 - spectra
    side_pad = jnp.zeros((spectra - first, pad), jnp.float32)
    foot = jnp.zeros((pad, 256), jnp.float32)
    packed = jnp.concatenate([pieces[0][:first], jnp.zeros((first, 128), jnp.float32)], axis=1)
    low_re = jnp.concatenate([packed, jnp.concatenate([wide[:, :spectra], side_pad], axis=1), foot], axis=0)
    row = lax.broadcasted_iota(jnp.int32, (256, 256), 0)
    col = lax.broadcasted_iota(jnp.int32, (256, 256), 1)
    turned = low_re.T
    k_re = jnp.where(row >= col, low_re, turned)
    low_im = jnp.concatenate(
        [-turned[:first], jnp.concatenate([wide[:, spectra:], side_pad], axis=1), foot], axis=0
    )
    k_im = jnp.where(row > col, low_im, jnp.where(row < col, -low_im.T, 0.0))
    w = [pieces[0][first : first + 2 * k, :first]]
    w += [piece[tiles * block : tiles * block + 2 * k, :block] for piece in pieces[1:]]
    w = jnp.concatenate(w + [jnp.zeros((2 * k, pad), jnp.float32)], axis=1)
    both = jnp.concatenate([k_re, k_im], axis=1)
    high = both.astype(jnp.bfloat16)
    rest = both - high.astype(jnp.float32)
    mid = rest.astype(jnp.bfloat16)
    low = (rest - mid.astype(jnp.float32)).astype(jnp.bfloat16)
    n2 = 2 * k
    a = jnp.zeros((n2, 256), jnp.float32)
    b = jnp.where(
        lax.broadcasted_iota(jnp.int32, (n2, 128), 0) == lax.broadcasted_iota(jnp.int32, (n2, 128), 1), 1.0, 0.0
    )
    b = jnp.where(lax.broadcasted_iota(jnp.int32, (n2, 128), 0) < k, b, 0.0)
    held = gram0
    for _ in range(ITERS):
        w3 = split3(w)
        on_high = plain(w3, high)
        on_mid = plain(w3[: 2 * n2], mid)
        on_low = plain(w3[:n2], low)
        kw = (on_low + on_mid[n2:] + on_high[2 * n2 :]) + (on_mid[:n2] + on_high[n2 : 2 * n2]) + on_high[:n2]
        on_re, on_im = kw[:, :256], kw[:, 256:]
        kw = jnp.concatenate([on_re[:k] + on_im[k:], on_re[k:] - on_im[:k]], axis=0)
        y = kw / spectra + loading * w
        u = (y + loading * w) / spectra
        g_re = exact(w, u[:k])
        g_im = exact(w, u[k:])
        gram = jnp.concatenate([g_re[:k] + g_im[k:], g_im[:k] - g_re[k:]], axis=0) + loading * loading * held
        grown = jnp.concatenate([y, w / spectra + loading * a, loading * b], axis=1)
        grown = eliminate(gram, grown, k)
        w, a, b = grown[:, :256], grown[:, 256:512], grown[:, 512:]
        held = b_identity(n2, k)
    return jnp.concatenate([w, a, b], axis=1)


def eliminate(gram, rows, k):
    g_re, g_im = gram[:k], -gram[k:]
    r_re, r_im = rows[:k], rows[k:]
    row = lax.broadcasted_iota(jnp.int32, (k, 1), 0)
    scale = jnp.zeros((k, 1), jnp.float32)
    for j in range(k):
        c_re, c_im = g_re[:, j : j + 1], g_im[:, j : j + 1]
        pivot = c_re[j : j + 1]
        scale = jnp.where(row == j, pivot, scale)
        if j == k - 1:
            break
        l_re = jnp.where(row > j, c_re / pivot, 0.0)
        l_im = jnp.where(row > j, c_im / pivot, 0.0)
        a_re, a_im = g_re[j : j + 1], g_im[j : j + 1]
        g_re, g_im = g_re - (l_re * a_re - l_im * a_im), g_im - (l_re * a_im + l_im * a_re)
        b_re, b_im = r_re[j : j + 1], r_im[j : j + 1]
        r_re, r_im = r_re - (l_re * b_re - l_im * b_im), r_im - (l_re * b_im + l_im * b_re)
    scale = 1.0 / jnp.sqrt(scale)
    return jnp.concatenate([r_re * scale, r_im * scale], axis=0)


def b_identity(n2, k):
    row = lax.broadcasted_iota(jnp.int32, (n2, k), 0)
    col = lax.broadcasted_iota(jnp.int32, (n2, k), 1)
    return jnp.where(row == col, 1.0, 0.0)


def finish_kernel(own_ref, q_ref, left_ref, out_ref):
    tile, _, chans, rows, cols = own_ref.shape
    block = rows // 2
    n2 = q_ref.shape[2]
    for c in range(chans):
        w3 = split3(left_ref[c])
        w_left = jnp.concatenate([w3[:n2], w3[:n2], w3[n2 : 2 * n2], w3[n2 : 2 * n2], w3[:n2], w3[2 * n2 :]], axis=0)
        for t in range(tile):
            s3 = split3(q_ref[t, c])
            s_right = jnp.concatenate(
                [s3[:n2], s3[n2 : 2 * n2], s3[:n2], s3[n2 : 2 * n2], s3[2 * n2 :], s3[:n2]], axis=0
            )
            cleaned = own_ref[t, 0, c].astype(jnp.float32) - tn(w_left, s_right)
            out_ref[0, c, :, t * cols : (t + 1) * cols] = cleaned[:block]
            out_ref[1, c, :, t * cols : (t + 1) * cols] = cleaned[block:]


def channelize_kernel(volts_ref, table_ref, out_ref):
    step = pl.program_id(0)
    span = (STEP + TAPS - 1) * P_SIZE
    start = pl.multiple_of(step * (STEP * P_SIZE), P_SIZE)
    chunk = volts_ref[:, pl.ds(start, span)]
    result = nt(table_ref[...], chunk)
    out_ref[...] = result.reshape(out_ref.shape).astype(jnp.bfloat16)


def channelize(voltages, table, rows, spectra_all):
    inputs_local, samples = voltages.shape
    return pl.pallas_call(
        channelize_kernel,
        grid=(spectra_all // STEP,),
        in_specs=[VMEM, VMEM],
        out_specs=pl.BlockSpec((rows, STEP, inputs_local), lambda i: (0, i, 0)),
        out_shape=jax.ShapeDtypeStruct((rows, spectra_all, inputs_local), jnp.bfloat16),
        compiler_params=pltpu.CompilerParams(vmem_limit_bytes=40 * 2**20),
    )(voltages, table)


def start_kernel(v_ref, q_ref, pg_ref, *, k, lanes):
    chans, _, spectra, _ = v_ref.shape
    pg_ref[...] = jnp.zeros_like(pg_ref)
    for c in range(chans):
        pg_ref[2 * k * c : 2 * k * (c + 1), :spectra] = project(q_ref[...], v_ref[c, 0], v_ref[c, 1], k)


def step_kernel(v_ref, z_ref, pg_ref, z_out, pg_out, *, k, lanes, first):
    chans, _, spectra, width = v_ref.shape
    pg_out[...] = jnp.zeros_like(pg_out)
    for c in range(chans):
        at = slice(2 * k * c, 2 * k * (c + 1))
        weights = pg_ref[at, :spectra]
        basis = z_ref[...] if first else z_ref[c]
        if not first:
            m_re, m_im = inverse_factor(pg_ref[at, lanes:], k)
            weights = mix(m_re, m_im, weights, k)
            basis = mix(m_re, m_im, basis, k)
        real_v, imag_v = v_ref[c, 0], v_ref[c, 1]
        parts = split3(weights / spectra)
        on_re = fold3(plain(parts, real_v))
        on_im = fold3(plain(parts, imag_v))
        z = jnp.concatenate([on_re[:k] - on_im[k:], on_re[k:] + on_im[:k]], axis=0) + loading * basis
        z_out[c] = z
        pg_out[at, :spectra] = project(z, real_v, imag_v, k)
        pad = jnp.zeros((lanes_pad(k), width), jnp.float32)
        right = jnp.concatenate([z[:k], pad], axis=0)
        right_im = jnp.concatenate([z[k:], pad], axis=0)
        dims = (((1,), (1,)), ((), ()))
        first_dot = lax.dot_general(z, right, dims, precision=highest, preferred_element_type=jnp.float32)
        second_dot = lax.dot_general(z, right_im, dims, precision=highest, preferred_element_type=jnp.float32)
        g_re = first_dot[:k] + second_dot[k:]
        g_im = second_dot[:k] - first_dot[k:]
        pg_out[at, lanes:] = jnp.concatenate([g_re, g_im], axis=0)


def lanes_pad(k):
    return 128 - k


def clean_kernel(v_ref, z_ref, pg_ref, out_ref, *, k, lanes):
    chans, _, spectra, width = v_ref.shape
    parts_count, _, _, block, _ = out_ref.shape
    for c in range(chans):
        at = slice(2 * k * c, 2 * k * (c + 1))
        m_re, m_im = inverse_factor(pg_ref[at, lanes:], k)
        w = mix(m_re, m_im, pg_ref[at, :spectra], k)
        q = mix(m_re, m_im, z_ref[c], k)
        turned = jnp.concatenate([q[k:], -q[:k]], axis=0)
        w3 = split3(w)
        n2 = 2 * k
        w_left = jnp.concatenate([w3[:n2], w3[:n2], w3[n2 : 2 * n2], w3[n2 : 2 * n2], w3[:n2], w3[2 * n2 :]], axis=0)
        for r, side in ((0, q), (1, turned)):
            s3 = split3(side)
            s_right = jnp.concatenate(
                [s3[:n2], s3[n2 : 2 * n2], s3[:n2], s3[n2 : 2 * n2], s3[2 * n2 :], s3[:n2]], axis=0
            )
            fitted = tn(w_left, s_right)
            cleaned = v_ref[c, r].astype(jnp.float32) - fitted
            out_ref[:, r, c] = cleaned.reshape(parts_count, block, width).astype(jnp.bfloat16)


def reduce_kernel(x_ref, out_ref, land_ref, send1, recv1, send2, recv2, *, size, chunk):
    me = lax.axis_index("tile")
    barrier = pltpu.get_barrier_semaphore()
    for d in range(1, size):
        peer = lax.rem(me + d, size)
        pl.semaphore_signal(barrier, inc=1, device_id={"tile": peer}, device_id_type=MESH)
    pl.semaphore_wait(barrier, size - 1)
    mine = pl.ds(pl.multiple_of(me * chunk, 8), chunk)
    sends = []
    for d in range(1, size):
        peer = lax.rem(me + d, size)
        copy = pltpu.make_async_remote_copy(
            src_ref=x_ref.at[pl.ds(pl.multiple_of(peer * chunk, 8), chunk)],
            dst_ref=land_ref.at[d - 1],
            send_sem=send1.at[d - 1],
            recv_sem=recv1.at[d - 1],
            device_id={"tile": peer},
            device_id_type=MESH,
        )
        copy.start()
        sends.append(copy)
    total = x_ref[mine]
    for d in range(1, size):
        sends[d - 1].wait_recv()
        total = total + land_ref[d - 1]
    out_ref[mine] = total
    later = []
    for d in range(1, size):
        peer = lax.rem(me + d, size)
        copy = pltpu.make_async_remote_copy(
            src_ref=out_ref.at[mine],
            dst_ref=out_ref.at[mine],
            send_sem=send2.at[d - 1],
            recv_sem=recv2.at[d - 1],
            device_id={"tile": peer},
            device_id_type=MESH,
        )
        copy.start()
        later.append(copy)
    for copy in later:
        copy.wait_recv()
    for copy in sends + later:
        copy.wait_send()


def tile_sum(x, size):
    rows, width = x.shape
    chunk = rows // size
    return pl.pallas_call(
        functools.partial(reduce_kernel, size=size, chunk=chunk),
        in_specs=[VMEM],
        out_specs=VMEM,
        out_shape=jax.ShapeDtypeStruct(x.shape, jnp.float32),
        scratch_shapes=[pltpu.VMEM((size - 1, chunk, width), jnp.float32)]
        + [pltpu.SemaphoreType.DMA((size - 1,))] * 4,
        compiler_params=pltpu.CompilerParams(collective_id=0, has_side_effects=True),
    )(x)


def up(value, unit):
    return -(-value // unit) * unit


def body_split(voltages, channel_ids, start_basis):
    inputs_local, samples_count = voltages.shape
    freq_count = lax.axis_size("freq")
    tile_count = lax.axis_size("tile")
    channels = channel_ids.shape[0]
    chan_local = channels // freq_count
    spectra_all = samples_count // P_SIZE - TAPS + 1
    spectra_local = spectra_all // tile_count
    k = start_basis.shape[1]
    width = freq_count * inputs_local

    coeffs = make_table(channel_ids, TAPS, P_SIZE).reshape(TAPS, 2 * channels, P_SIZE)
    local = channelize(voltages, banded(coeffs), 2 * channels, spectra_all)
    parcel = local.reshape(2, freq_count, chan_local, spectra_all, inputs_local)
    arrived = lax.all_to_all(parcel, "freq", split_axis=1, concat_axis=1, tiled=True)
    values = jnp.transpose(arrived, (2, 0, 3, 1, 4)).reshape(chan_local, 2, spectra_all, width)

    mine = lax.axis_index("tile")
    start = start_basis.reshape(2 * k, freq_count, tile_count, inputs_local)
    start = lax.dynamic_index_in_dim(start, mine, 2, keepdims=False).reshape(2 * k, width)

    lanes = up(spectra_all, 128)
    chunk = up(-(-chan_local * 2 * k // tile_count), 8)
    packed = jax.ShapeDtypeStruct((tile_count * chunk, lanes + 128), jnp.float32)
    z_shape = jax.ShapeDtypeStruct((chan_local, 2 * k, width), jnp.float32)
    params = pltpu.CompilerParams(vmem_limit_bytes=40 * 2**20)

    partial = pl.pallas_call(
        functools.partial(start_kernel, k=k, lanes=lanes),
        in_specs=[VMEM] * 2, out_specs=VMEM, out_shape=packed, compiler_params=params,
    )(values, start)
    z = start
    for step_at in range(ITERS):
        total = tile_sum(partial, tile_count)
        z, partial = pl.pallas_call(
            functools.partial(step_kernel, k=k, lanes=lanes, first=step_at == 0),
            in_specs=[VMEM] * 3, out_specs=[VMEM] * 2, out_shape=[z_shape, packed],
            compiler_params=params,
        )(values, z, total)
    total = tile_sum(partial, tile_count)
    cleaned = pl.pallas_call(
        functools.partial(clean_kernel, k=k, lanes=lanes),
        in_specs=[VMEM] * 3, out_specs=VMEM,
        out_shape=jax.ShapeDtypeStruct((tile_count, 2, chan_local, spectra_local, width), jnp.bfloat16),
        compiler_params=params,
    )(values, z, total)
    moved = lax.all_to_all(cleaned, "tile", split_axis=0, concat_axis=0, tiled=True)
    moved = moved.reshape(tile_count, 2, chan_local, spectra_local, freq_count, inputs_local)
    moved = jnp.transpose(moved, (1, 2, 3, 4, 0, 5)).astype(jnp.float32)
    return moved.reshape(2, chan_local, spectra_local, freq_count * tile_count * inputs_local)


def body(voltages, channel_ids, start_basis):
    inputs_local, samples_count = voltages.shape
    freq_count = lax.axis_size("freq")
    tile_count = lax.axis_size("tile")
    if inputs_local % 128:
        return body_split(voltages, channel_ids, start_basis)
    channels = channel_ids.shape[0]
    chan_local = channels // freq_count
    spectra_all = samples_count // P_SIZE - TAPS + 1
    spectra_local = spectra_all // tile_count
    k = start_basis.shape[1]
    width = freq_count * inputs_local
    if spectra_all != 192 or spectra_local % SUB or tile_count % 4 or tile_count <= 128 // spectra_local or chan_local > 4 or k != 8:
        return body_split(voltages, channel_ids, start_basis)

    start = start_basis.reshape(2 * k, freq_count * tile_count * inputs_local)
    rows = 2 * spectra_local
    line = tile_count // 2
    stages, heights, _, first = plan(spectra_all, spectra_local, k)
    half, count = sum(heights), len(stages)
    sem = pltpu.SemaphoreType.DMA
    peers = freq_count - 1
    own, q, left = pl.pallas_call(
        functools.partial(fused_kernel, k=k, freq=freq_count, tile=tile_count),
        in_specs=[pl.BlockSpec(memory_space=pl.ANY), pl.BlockSpec(memory_space=pltpu.SMEM), VMEM],
        out_specs=[pl.BlockSpec(memory_space=pl.ANY), VMEM, VMEM],
        out_shape=[
            jax.ShapeDtypeStruct((tile_count, freq_count, chan_local, rows, inputs_local), jnp.bfloat16),
            jax.ShapeDtypeStruct((tile_count, chan_local, 2 * k, width), jnp.float32),
            jax.ShapeDtypeStruct((chan_local, 2 * k, rows), jnp.float32),
        ],
        scratch_shapes=[
            pltpu.VMEM((tile_count, inputs_local, (spectra_local + TAPS - 1) * P_SIZE), jnp.bfloat16),
            pltpu.VMEM((2 * channels * SUB, (SUB + TAPS - 1) * P_SIZE), jnp.bfloat16),
            pltpu.VMEM((tile_count, freq_count, chan_local, rows, inputs_local), jnp.bfloat16),
            pltpu.VMEM((tile_count, freq_count, chan_local, rows, inputs_local), jnp.bfloat16),
            pltpu.VMEM((chan_local, 2, spectra_all, width), jnp.bfloat16),
            pltpu.VMEM((chan_local, 2, half, 128), jnp.float32),
            pltpu.VMEM((chan_local, half, 128), jnp.float32),
            pltpu.VMEM((chan_local, half, 128), jnp.float32),
            pltpu.VMEM((chan_local, line - 1, half, 128), jnp.float32),
            pltpu.VMEM((2, half, 128), jnp.float32),
            pltpu.VMEM((chan_local, 2 * k, 640), jnp.float32),
            sem((tile_count,)), sem((tile_count,)), sem((freq_count,)),
            sem((tile_count, peers)), sem((tile_count, peers)),
            sem((tile_count, freq_count)), sem((tile_count, freq_count)),
            sem((count, chan_local)), sem((count, chan_local)),
            sem((count, chan_local)), sem((count, chan_local, line - 1)),
            sem((count, chan_local)), sem((count, chan_local)),
            sem((tile_count - 1,)), sem((chan_local,)),
            sem((chan_local, line - 1)), sem((chan_local, line)),
            sem((chan_local, line)), sem((chan_local, line)),
        ],
        compiler_params=pltpu.CompilerParams(
            collective_id=0, has_side_effects=True, vmem_limit_bytes=56 * 2**20
        ),
    )(voltages, channel_ids, start)
    stride = tile_count * inputs_local
    return pl.pallas_call(
        finish_kernel,
        grid=(freq_count,),
        in_specs=[
            pl.BlockSpec((tile_count, 1, chan_local, rows, inputs_local), lambda f: (0, f, 0, 0, 0)),
            pl.BlockSpec((tile_count, chan_local, 2 * k, inputs_local), lambda f: (0, 0, 0, f)),
            pl.BlockSpec((chan_local, 2 * k, rows), lambda f: (0, 0, 0)),
        ],
        out_specs=pl.BlockSpec((2, chan_local, spectra_local, stride), lambda f: (0, 0, 0, f)),
        out_shape=jax.ShapeDtypeStruct((2, chan_local, spectra_local, freq_count * stride), jnp.float32),
        compiler_params=pltpu.CompilerParams(vmem_limit_bytes=60 * 2**20),
    )(own, q, left)


def solution(mesh):
    in_specs = (P(("freq", "tile"), None), P(), P())
    out_specs = P(None, "freq", "tile", None)
    return jax.shard_map(body, mesh=mesh, in_specs=in_specs, out_specs=out_specs, check_vma=False)
```
